32 devices in a mesh: gx: 8 (over y, x, core), gy: 4 (over z).
Axes of the slice: x: 2, y: 2, z: 4, core: 2. Of those that a mesh axis runs over, the one named last changes fastest.
Arguments:
- density: bfloat16 [256, 128, 128], P('gx', 'gy'), may hold values from 0.29882812 to 1.1953125
- vel_x: float32 [256, 128, 128], P('gx', 'gy'), may hold values from -6 to 6
- vel_y: float32 [256, 128, 128], P('gx', 'gy'), may hold values from -6 to 6
- vel_z: float32 [256, 128, 128], P('gx', 'gy'), may hold values from -6 to 6
- z_modes: float32 [128, 128], replicated, may hold values from -1 to 1, as said below
- z_stiffness: float32 [128], replicated, may hold values from 0.0005 to 0.5
Outputs:
- new_x: float32 [256, 128, 128], P('gx', 'gy')
- new_y: float32 [256, 128, 128], P('gx', 'gy')
- new_z: float32 [256, 128, 128], P('gx', 'gy')
The draws below stay inside these ranges and needn't reach their ends.
Inputs may be any that keep to these rules, and one draw needn't show every extreme that they name: z_modes is an orthogonal matrix.
All inputs are finite; a program needn't handle non-finite values.
Results may differ from the reference program's by a relative error of at most 0.00055.
Values sent between devices are 32-bit elements; how exact they have to be, the bound alone decides.
No kernel may reach another device: no remote copies, remote signals or barrier semaphores. Data moves between devices by JAX's collectives and lax.ppermute only.
A program may use at most 64 MiB of HBM per device.

```python
import math
import jax
import jax.numpy as jnp
from jax import lax

NZ = 128
NX = 256
NY = 128


def draw_z_modes(key, part):
    matrix = jax.random.normal(jax.random.fold_in(key, 17), (NZ, NZ), jnp.float32)
    q_factor, r_factor = jnp.linalg.qr(matrix)
    return q_factor.astype(jnp.float32)


def block_levels(key, dims, shards, smallest, largest):
    factor_of, own = 1.0, jax.random.fold_in(key, 6)
    for dim, parts in shards:
        draws = jnp.exp(jax.random.uniform(jax.random.fold_in(own, dim), (parts,), jnp.float32, smallest / len(shards), largest / len(shards)))
        factor_of = factor_of * jnp.repeat(draws, dims[dim] // parts).reshape([-1 if axis == dim else 1 for axis in range(len(dims))])
    return factor_of


def normal_values(stream_key, extent, scale, bound, shards=(), kind=jnp.bfloat16):
    level = block_levels(stream_key, extent, shards, -0.22, 0.18) if shards else 1.0
    entries = jax.random.normal(stream_key, extent, jnp.float32) * scale * level
    return jnp.minimum(jnp.maximum(entries, -bound), bound).astype(kind)


def setup_inputs(seed: int = 0) -> dict:
    arg_keys = jax.random.split(jax.random.key(seed), 7)
    density = jnp.clip(jnp.exp(math.log(1.1953125) - 1.3862944 * jax.random.uniform(arg_keys[0], (NX, NY, NZ), jnp.float32) ** block_levels(arg_keys[0], (NX, NY, NZ), ((0, 8), (1, 4)), -0.2, 0.2)), 0.29882812, 1.1953125).astype(jnp.bfloat16)
    vel_x = normal_values(arg_keys[1], (NX, NY, NZ), 1.0, 6.0, ((0, 8), (1, 4)), jnp.float32)
    vel_y = normal_values(arg_keys[2], (NX, NY, NZ), 1.0, 6.0, ((0, 8), (1, 4)), jnp.float32)
    vel_z = normal_values(arg_keys[3], (NX, NY, NZ), 1.0, 6.0, ((0, 8), (1, 4)), jnp.float32)
    z_modes = draw_z_modes(jax.random.fold_in(arg_keys[6], 71), 0)
    z_stiffness = jnp.clip(jnp.exp(jax.random.uniform(arg_keys[5], (NZ,), jnp.float32, math.log(0.0005), math.log(0.5))), 0.0005, 0.5)
    return {"density": density, "vel_x": vel_x, "vel_y": vel_y, "vel_z": vel_z, "z_modes": z_modes, "z_stiffness": z_stiffness}


def lower_step(values, axis):
    moved = jnp.moveaxis(values, axis, -1)
    padding = [(0, 0)] * (moved.ndim - 1) + [(1, 0)]
    result = moved - jnp.pad(moved[..., :-1], padding)
    return jnp.moveaxis(result, -1, axis)

def upper_step(values, axis):
    moved = jnp.moveaxis(values, axis, -1)
    padding = [(0, 0)] * (moved.ndim - 1) + [(0, 1)]
    result = jnp.pad(moved[..., 1:], padding) - moved
    return jnp.moveaxis(result, -1, axis)

def cosine_forward(values):
    length = values.shape[-1]
    folded = jnp.concatenate([values[..., 0::2], values[..., 1::2][..., ::-1]], -1)
    spectrum = jnp.fft.fft(folded, axis=-1)
    modes = jnp.arange(length)
    angle = -jnp.pi * modes / (2 * length)
    scales = jnp.where(modes == 0, jnp.sqrt(1.0 / length), jnp.sqrt(2.0 / length))
    result = spectrum.real * jnp.cos(angle) - spectrum.imag * jnp.sin(angle)
    return (result * scales).astype(values.dtype)

def cosine_inverse(values):
    length = values.shape[-1]
    half_len = length // 2
    modes = jnp.arange(length)
    angle = jnp.pi * modes / (2 * length)
    scales = jnp.where(modes == 0, jnp.sqrt(1.0 / length), jnp.sqrt(2.0 / length))
    weighted = values * scales
    twisted = lax.complex(weighted * jnp.cos(angle), weighted * jnp.sin(angle))
    folded = jnp.fft.ifft(twisted, axis=-1).real * length
    paired = jnp.stack([folded[..., :half_len], folded[..., ::-1][..., :half_len]], -1)
    return paired.reshape(values.shape).astype(values.dtype)

def plane_forward(plane):
    along_x = cosine_forward(plane.T).T
    return cosine_forward(along_x)

def plane_inverse(plane):
    along_y = cosine_inverse(plane)
    return cosine_inverse(along_y.T).T

def reference(density, vel_x, vel_y, vel_z, z_modes, z_stiffness):
    heaviness = density.astype(jnp.float32)
    momentum_x = heaviness * vel_x
    momentum_y = heaviness * vel_y
    momentum_z = heaviness * vel_z
    source = lower_step(momentum_x, 0) + lower_step(momentum_y, 1) + lower_step(momentum_z, 2)
    planes = jnp.transpose(source, (2, 0, 1))
    spectrum = lax.map(plane_forward, planes)
    spectrum = jnp.einsum('zab,zk->kab', spectrum, z_modes, precision=lax.Precision.HIGHEST)
    modes_x = jnp.arange(NX).astype(jnp.float32)
    modes_y = jnp.arange(NY).astype(jnp.float32)
    eigen_x = -(2.0 - 2.0 * jnp.cos(jnp.pi * modes_x / NX))
    eigen_y = -(2.0 - 2.0 * jnp.cos(jnp.pi * modes_y / NY))
    divisor = eigen_x[None, :, None] + eigen_y[None, None, :] - z_stiffness[:, None, None]
    pressure_hat = spectrum / divisor
    planes_back = jnp.einsum('kab,zk->zab', pressure_hat, z_modes, precision=lax.Precision.HIGHEST)
    pressure = jnp.transpose(lax.map(plane_inverse, planes_back), (1, 2, 0))
    new_x = vel_x - upper_step(pressure, 0) / heaviness
    new_y = vel_y - upper_step(pressure, 1) / heaviness
    new_z = vel_z - upper_step(pressure, 2) / heaviness
    return (new_x, new_y, new_z)
```

```python
import functools
import math

import jax
import jax.numpy as jnp
import numpy as np
from jax import lax
from jax.experimental import pallas as pl
from jax.experimental.pallas import tpu as pltpu
from jax.sharding import PartitionSpec as P

HIGHEST = lax.Precision.HIGHEST
F32 = jnp.float32
BF16 = jnp.bfloat16
GROUP = 8


def cosine(length):
    rows = np.arange(length)[:, None]
    cols = np.arange(length)[None, :]
    table = np.sqrt(2.0 / length) * np.cos(np.pi * rows * (2 * cols + 1) / (2 * length))
    table[0] = math.sqrt(1.0 / length)
    return table


def eigen(length):
    return -4.0 * np.sin(np.pi * np.arange(length) / (2 * length)) ** 2


def halves(table):
    table = np.asarray(table, np.float64)
    high = table.astype(np.float32).astype(BF16)
    low = (table - high.astype(np.float64)).astype(np.float32).astype(BF16)
    return np.stack([high, low])


def sine(length):
    modes = np.arange(1, length + 1)
    return np.sqrt(2.0 / (length + 1)) * np.sin(np.pi * np.outer(modes, modes) / (length + 1))


def wall_eigen(length):
    return -4.0 * np.sin(np.pi * np.arange(1, length + 1) / (2 * (length + 1))) ** 2


def local_tables(bx, by):
    sx, sy = sine(bx), sine(by)
    along_y = np.kron(np.eye(GROUP), sy)
    along_x = np.kron(sx, np.eye(GROUP))
    faces = np.concatenate(
        [
            np.einsum("a,by->yab", sx[:, -1], sy),
            np.einsum("a,by->yab", sx[:, 0], sy),
            np.einsum("ax,b->xab", sx, sy[:, -1]),
            np.einsum("ax,b->xab", sx, sy[:, 0]),
        ]
    )
    count = faces.shape[0]
    faces = faces.reshape(count, bx, by // GROUP, GROUP).transpose(2, 0, 1, 3)
    faces = faces.reshape(by // GROUP, count, bx * GROUP)
    return along_y, along_x, faces, -faces.transpose(0, 2, 1)


def edge_rows(blocks, size):
    table = cosine(blocks * size)
    ahead = np.minimum(size * (np.arange(blocks) + 1), blocks * size - 1)
    behind = np.maximum(size * np.arange(blocks) - 1, 0)
    return table[:, ahead].T, table[:, behind].T


def phase_tables(blocks, size):
    total = blocks * size
    modes = np.arange(total)
    scale = np.where(modes == 0, math.sqrt(1.0 / total), math.sqrt(2.0 / total))
    near = np.pi * np.outer(2 * np.arange(size) + 1, modes) / (2 * total)
    far = np.pi * np.outer(np.arange(blocks), modes) * size / total
    near = np.concatenate([scale * np.cos(near), scale * np.sin(near)], 1)
    return near, np.cos(far), np.sin(far)


def split(values):
    high = values.astype(BF16)
    low = (values - high.astype(F32)).astype(BF16)
    return high, low


def mm(left, right, dims=((1,), (0,))):
    def one(a, b):
        return lax.dot_general(a, b, (dims, ((), ())), preferred_element_type=F32)

    return one(left[0], right[0]) + (one(left[0], right[1]) + one(left[1], right[0]))


def pair(ref, *index):
    return ref[(0, *index)], ref[(1, *index)]


def iota(shape, dim):
    return lax.broadcasted_iota(jnp.int32, shape, dim)


def first_kernel(
    gx, gy, rho_ref, vx_ref, vy_ref, vz_ref, zm_ref, zs_ref, ex_ref, ey_ref,
    ay_ref, ax_ref, face_ref, hat_ref, out_ref, stage, edge,
):
    bx, by, nz = vx_ref.shape
    cut_x = (lax.axis_index("gx") < gx - 1).astype(F32)
    cut_y = (lax.axis_index("gy") < gy - 1).astype(F32)
    row = iota((by, nz), 0)
    lane = iota((by, nz), 1)
    zm = split(zm_ref[...])
    previous = None
    for start in range(0, bx, GROUP):
        layers = []
        for x in range(start, start + GROUP):
            rho = rho_ref[x].astype(F32)
            mx = rho * vx_ref[x]
            my = rho * vy_ref[x]
            mz = rho * vz_ref[x]
            total = mx if previous is None else mx - previous
            previous = mx
            below = jnp.where(row == 0, 0.0, pltpu.roll(my, 1, 0))
            total = total + (my - below)
            under = jnp.where(lane == 0, 0.0, pltpu.roll(mz, 1, 1))
            total = total + (mz - under)
            layers.append(total)
            edge[by + x : by + x + 1, :] = my[by - 1 :, :] * cut_y
            if x == bx - 1:
                edge[0:by, :] = mx * cut_x
        block = jnp.concatenate(layers, 0)
        block = mm(split(block), zm)
        block = mm(pair(ay_ref), split(block))
        stage[start : start + GROUP] = block.reshape(GROUP, by, nz)
    traces = None
    for group in range(by // GROUP):
        rows = slice(group * GROUP, (group + 1) * GROUP)
        block = stage[:, rows, :].reshape(bx * GROUP, nz)
        block = mm(pair(ax_ref), split(block)).reshape(bx, GROUP, nz)
        hat_ref[:, rows, :] = block
        divisor = ex_ref[...] + ey_ref[rows, :][None] - zs_ref[...][None]
        block = (block / divisor).reshape(bx * GROUP, nz)
        part = mm(pair(face_ref, group), split(block))
        traces = part if traces is None else traces + part
    momentum = mm(split(edge[...]), zm)
    mxs, mys = momentum[:by], momentum[by:]
    traces = traces + jnp.concatenate(
        [mxs, jnp.zeros_like(mxs), mys, jnp.zeros_like(mys)], 0
    )
    turned = traces.T
    each = out_ref.shape[1]
    for peer in range(out_ref.shape[0]):
        out_ref[peer] = turned[peer * each : (peer + 1) * each, :]


def middle_kernel(
    gx, gy, bx, by, in_ref, zs_ref, ex_ref, ey_ref, nx_ref, ny_ref, nxt_ref, nyt_ref,
    far_x_ref, far_y_ref, uxt_ref, uy_ref, ux_ref, out_ref,
):
    peers, each, lanes = in_ref.shape
    me = lax.axis_index("gx") * gy + lax.axis_index("gy")
    total_x, total_y = gx * bx, gy * by
    row = iota((peers, lanes), 0)
    lane = iota((peers, lanes), 1)
    row_x, row_y = row // gy, row % gy
    blocks = [in_ref[:, c, :] for c in range(each)]
    xs, ys = [], []
    for block in blocks:
        xs += [block[:, 0:by], block[:, by : 2 * by]]
        ys += [block[:, 2 * by : 2 * by + bx], block[:, 2 * by + bx :]]
    wave_x = mm(split(jnp.concatenate(xs, 0)), pair(nx_ref))
    wave_y = mm(split(jnp.concatenate(ys, 0)), pair(ny_ref))
    far_xc, far_xs = far_x_ref[0], far_x_ref[1]
    far_yc, far_ys = far_y_ref[0], far_y_ref[1]
    out_x, out_y = [], []
    for c in range(each):
        rows = slice(2 * peers * c, 2 * peers * (c + 1))
        wx = wave_x[rows, :total_y] * far_xc - wave_x[rows, total_y:] * far_xs
        wy = wave_y[rows, :total_x] * far_yc - wave_y[rows, total_x:] * far_ys
        spectrum = mm(pair(uxt_ref), split(wx)) + mm(split(wy.T), pair(uy_ref))
        spectrum = spectrum / (ex_ref[...] + ey_ref[...] - zs_ref[me * each + c])
        parts = split(spectrum)
        vx = mm(pair(ux_ref), parts)
        vy = mm(pair(uy_ref), parts, ((1,), (1,)))
        out_x.append(jnp.concatenate([vx * far_xc, -vx * far_xs], 1))
        out_y.append(jnp.concatenate([vy * far_yc, -vy * far_ys], 1))
    back_x = mm(split(jnp.concatenate(out_x, 0)), pair(nxt_ref))
    back_y = mm(split(jnp.concatenate(out_y, 0)), pair(nyt_ref))
    face = jnp.where(lane < by, 0, jnp.where(lane < 2 * by, 1, jnp.where(lane < 2 * by + bx, 2, 3)))
    coord = jnp.where(face < 2, row_x, row_y)
    end = jnp.where(face < 2, gx - 1, gy - 1)
    cut = jnp.where(face % 2 == 0, end - coord, coord) > 0
    for c in range(each):
        block = blocks[c]
        ahead_x = pltpu.roll(pltpu.roll(block, peers - gy, 0), lanes - by, 1)
        behind_x = pltpu.roll(pltpu.roll(block, gy, 0), by, 1)
        ahead_y = pltpu.roll(pltpu.roll(block, peers - 1, 0), lanes - bx, 1)
        behind_y = pltpu.roll(pltpu.roll(block, 1, 0), bx, 1)
        across = jnp.where(
            face == 0, ahead_x,
            jnp.where(face == 1, behind_x, jnp.where(face == 2, ahead_y, behind_y)),
        )
        across = jnp.where(cut, across, block)
        base = 2 * peers * c
        extra = jnp.concatenate(
            [
                back_x[base : base + peers], back_x[base + peers : base + 2 * peers],
                back_y[base : base + peers], back_y[base + peers : base + 2 * peers],
            ],
            1,
        )
        out_ref[:, c, :] = across - extra


def last_kernel(
    gx, gy, flux_ref, hat_ref, rho_ref, vx_ref, vy_ref, vz_ref, zm_ref, zs_ref, ex_ref, ey_ref,
    ay_ref, ax_ref, back_ref, ox_ref, oy_ref, oz_ref, stage,
):
    bx, by, nz = vx_ref.shape
    last_x = lax.axis_index("gx") == gx - 1
    last_y = lax.axis_index("gy") == gy - 1
    zt = split(zm_ref[...].T)
    each = flux_ref.shape[1]
    flux = jnp.concatenate([flux_ref[peer] for peer in range(flux_ref.shape[0])], 0).T
    flux_parts = split(flux)
    for group in range(by // GROUP):
        rows = slice(group * GROUP, (group + 1) * GROUP)
        block = hat_ref[:, rows, :].reshape(bx * GROUP, nz) + mm(pair(back_ref, group), flux_parts)
        divisor = ex_ref[...] + ey_ref[rows, :][None] - zs_ref[...][None]
        block = (block.reshape(bx, GROUP, nz) / divisor).reshape(bx * GROUP, nz)
        stage[:, rows, :] = mm(pair(ax_ref), split(block)).reshape(bx, GROUP, nz)
    for start in range(0, bx, GROUP):
        block = stage[start : start + GROUP].reshape(GROUP * by, nz)
        block = mm(pair(ay_ref), split(block))
        stage[start : start + GROUP] = mm(split(block), zt).reshape(GROUP, by, nz)
    edges = mm(split(jnp.concatenate([flux[:by], flux[2 * by : 2 * by + bx]], 0)), zt)
    row = iota((by, nz), 0)
    lane = iota((by, nz), 1)
    here = stage[0]
    for x in range(bx):
        rho = rho_ref[x].astype(F32)
        velocity = vx_ref[x]
        if x < bx - 1:
            following = stage[x + 1]
            ox_ref[x] = velocity - (following - here) / rho
        else:
            following = None
            step = jnp.where(last_x, 0.0, edges[:by]) - here
            ox_ref[x] = velocity - step / rho
        velocity = vy_ref[x]
        cut = jnp.broadcast_to(edges[by + x : by + x + 1, :], (by, nz))
        cut = jnp.where(last_y, 0.0, cut)
        step = jnp.where(row == by - 1, cut, pltpu.roll(here, by - 1, 0)) - here
        oy_ref[x] = velocity - step / rho
        step = jnp.where(lane == nz - 1, 0.0, pltpu.roll(here, nz - 1, 1)) - here
        oz_ref[x] = vz_ref[x] - step / rho
        here = following


def call(kernel, outs, scratch, args, smem=()):
    specs = [
        pl.BlockSpec(memory_space=pltpu.SMEM if i in smem else pltpu.VMEM)
        for i in range(len(args))
    ]
    return pl.pallas_call(
        kernel,
        out_shape=[jax.ShapeDtypeStruct(shape, F32) for shape in outs],
        in_specs=specs,
        out_specs=[pl.BlockSpec(memory_space=pltpu.VMEM)] * len(outs),
        scratch_shapes=[pltpu.VMEM(shape, F32) for shape in scratch],
    )(*args)


def by_faces(density, vel_x, vel_y, vel_z, z_modes, z_stiffness):
    bx, by, nz = vel_x.shape
    gx, gy = lax.axis_size("gx"), lax.axis_size("gy")
    peers = gx * gy
    each = nz // peers
    lanes = 2 * (bx + by)
    along_y, along_x, faces, back = local_tables(bx, by)
    f32 = lambda table: np.asarray(table, np.float32)
    ex = f32(np.broadcast_to(wall_eigen(bx)[:, None, None], (bx, 1, nz)))
    ey = f32(np.broadcast_to(wall_eigen(by)[:, None], (by, nz)))
    stiff = z_stiffness.reshape(1, nz)
    hat, sent = call(
        functools.partial(first_kernel, gx, gy),
        [(bx, by, nz), (peers, each, lanes)],
        [(bx, by, nz), (bx + by, nz)],
        (density, vel_x, vel_y, vel_z, z_modes, stiff, ex, ey,
         halves(along_y), halves(along_x), halves(faces)),
    )
    got = lax.all_to_all(sent, ("gx", "gy"), 0, 0, tiled=True)

    near_x, cos_x, sin_x = phase_tables(gy, by)
    near_y, cos_y, sin_y = phase_tables(gx, bx)
    row_x, row_y = np.arange(peers) // gy, np.arange(peers) % gy
    twice = lambda table: np.concatenate([table, table], 0)
    far_x = f32(np.stack([twice(cos_x[row_y]), twice(sin_x[row_y])]))
    far_y = f32(np.stack([twice(cos_y[row_x]), twice(sin_y[row_x])]))
    ahead_x, behind_x = edge_rows(gx, bx)
    ahead_y, behind_y = edge_rows(gy, by)
    ux = np.concatenate([ahead_x[row_x], behind_x[row_x]], 0)
    uy = np.concatenate([ahead_y[row_y], behind_y[row_y]], 0)
    total_x, total_y = gx * bx, gy * by
    (solved,) = call(
        functools.partial(middle_kernel, gx, gy, bx, by),
        [(peers, each, lanes)],
        [],
        (got, z_stiffness,
         f32(np.broadcast_to(eigen(total_x)[:, None], (total_x, total_y))),
         f32(eigen(total_y)[None, :]),
         halves(near_x), halves(near_y), halves(near_x.T), halves(near_y.T),
         far_x, far_y, halves(ux.T), halves(uy), halves(ux)),
        smem=(1,),
    )
    flux = lax.all_to_all(solved, ("gx", "gy"), 0, 0, tiled=True)
    return call(
        functools.partial(last_kernel, gx, gy),
        [(bx, by, nz)] * 3,
        [(bx, by, nz)],
        (flux, hat, density, vel_x, vel_y, vel_z, z_modes, stiff, ex, ey,
         halves(along_y), halves(along_x), halves(back)),
    )


def from_behind(block, axis, distance):
    devices = range(lax.axis_size(axis))
    route = [(i - distance, i) for i in devices if i - distance in devices]
    return lax.ppermute(block, axis, route)


def cosine_table(length):
    rows = lax.broadcasted_iota(jnp.int32, (length, length), 0)
    cols = lax.broadcasted_iota(jnp.int32, (length, length), 1)
    phase = rows * (2 * cols + 1) % (4 * length)
    angle = phase.astype(jnp.float32) * (math.pi / (2 * length))
    scales = jnp.where(rows == 0, math.sqrt(1.0 / length), math.sqrt(2.0 / length))
    return scales * jnp.cos(angle)


def upper_step(values):
    padding = [(0, 0)] * (values.ndim - 1) + [(0, 1)]
    return jnp.pad(values[..., 1:], padding) - values


def lower_step(values):
    padding = [(0, 0)] * (values.ndim - 1) + [(1, 0)]
    return values - jnp.pad(values[..., :-1], padding)


def eigenvalues(modes, length):
    return -(2.0 - 2.0 * jnp.cos(jnp.pi * modes / length))


def by_transposes(density, vel_x, vel_y, vel_z, z_modes, z_stiffness):
    cells_x = vel_x.shape[0]
    cells_y = vel_x.shape[1]
    depth = vel_x.shape[2]
    groups_x = lax.axis_size("gx")
    groups_y = lax.axis_size("gy")
    total_x = cells_x * groups_x
    total_y = cells_y * groups_y
    planes_dev = depth // groups_x
    xmodes_dev = total_x // groups_y
    table_x = cosine_table(total_x)
    table_y = cosine_table(total_y)
    heaviness = density.astype(jnp.float32)
    momentum_x = heaviness * vel_x
    momentum_y = heaviness * vel_y
    momentum_z = heaviness * vel_z
    below_x = from_behind(momentum_x[cells_x - 1 :], "gx", 1)
    below_y = from_behind(momentum_y[:, cells_y - 1 :], "gy", 1)
    diff_x = momentum_x - jnp.concatenate([below_x, momentum_x[:-1]], 0)
    diff_y = momentum_y - jnp.concatenate([below_y, momentum_y[:, :-1]], 1)
    source = diff_x + diff_y + lower_step(momentum_z)
    vertical = jnp.dot(source.reshape(cells_x * cells_y, depth), z_modes, precision=HIGHEST)
    vertical = vertical.reshape(cells_x, cells_y, groups_x, planes_dev).transpose(0, 2, 1, 3)
    vertical = vertical.reshape(cells_x, groups_x, cells_y * planes_dev)
    lines_x = lax.all_to_all(vertical, "gx", split_axis=1, concat_axis=0, tiled=True)
    lines_x = lines_x.reshape(total_x, cells_y, planes_dev)
    mixed = jnp.einsum("xyk,ax->yak", lines_x, table_x, precision=HIGHEST)
    mixed = mixed.reshape(cells_y, groups_y, xmodes_dev * planes_dev)
    lines_y = lax.all_to_all(mixed, "gy", split_axis=1, concat_axis=0, tiled=True)
    right_side = lines_y.reshape(total_y, xmodes_dev * planes_dev)
    spectrum = jnp.dot(table_y, right_side, precision=HIGHEST)
    z_first = lax.axis_index("gx") * planes_dev
    stiff_dev = lax.dynamic_slice_in_dim(z_stiffness, z_first, planes_dev)
    x_first = lax.axis_index("gy") * xmodes_dev
    modes_x = (x_first + jnp.arange(xmodes_dev, dtype=jnp.int32)).astype(jnp.float32)
    modes_y = jnp.arange(total_y, dtype=jnp.int32).astype(jnp.float32)
    divisor = (
        eigenvalues(modes_x, total_x)[None, :, None]
        + eigenvalues(modes_y, total_y)[:, None, None]
        - stiff_dev[None, None, :]
    )
    pressure_hat = spectrum / divisor.reshape(total_y, xmodes_dev * planes_dev)
    y_space = jnp.einsum("by,bc->yc", table_y, pressure_hat, precision=HIGHEST)
    modes_split = z_modes.reshape(depth, groups_x, planes_dev)
    sent_y = y_space.reshape(total_y, 1, xmodes_dev * planes_dev)
    lines_back = lax.all_to_all(sent_y, "gy", split_axis=0, concat_axis=1, tiled=True)
    lines_back = lines_back.reshape(cells_y, total_x, planes_dev)
    space_x = jnp.einsum("yak,ax->xyk", lines_back, table_x, precision=HIGHEST)
    sent_x = space_x.reshape(total_x, 1, cells_y * planes_dev)
    blocks = lax.all_to_all(sent_x, "gx", split_axis=0, concat_axis=1, tiled=True)
    blocks = blocks.reshape(cells_x, groups_x, cells_y, planes_dev)
    pressure = jnp.einsum("xhyk,zhk->xyz", blocks, modes_split, precision=HIGHEST)
    rim_x = from_behind(pressure[0:1], "gx", -1)
    grad_x = jnp.concatenate([pressure[1:], rim_x], 0) - pressure
    rim_y = from_behind(pressure[:, 0:1], "gy", -1)
    grad_y = jnp.concatenate([pressure[:, 1:], rim_y], 1) - pressure
    grad_z = upper_step(pressure)
    new_x = vel_x - grad_x / heaviness
    new_y = vel_y - grad_y / heaviness
    new_z = vel_z - grad_z / heaviness
    return (new_x, new_y, new_z)


def solution(mesh):
    sizes = mesh.shape
    peers = sizes["gx"] * sizes["gy"]

    def local(density, vel_x, vel_y, vel_z, z_modes, z_stiffness):
        cells_x, cells_y, depth = vel_x.shape
        fits = depth % peers == 0 and depth % 128 == 0
        fits = fits and cells_x % GROUP == 0 and cells_y % GROUP == 0
        fits = fits and 2 * (cells_x + cells_y) % 128 == 0
        plan = by_faces if fits else by_transposes
        return tuple(plan(density, vel_x, vel_y, vel_z, z_modes, z_stiffness))

    block = P("gx", "gy", None)
    return jax.shard_map(
        local,
        mesh=mesh,
        in_specs=(block, block, block, block, P(), P()),
        out_specs=(block, block, block),
        check_vma=False,
    )
```

```python
import functools
import math

import jax
import jax.numpy as jnp
import numpy as np
from jax import lax
from jax.experimental import pallas as pl
from jax.experimental.pallas import tpu as pltpu
from jax.sharding import PartitionSpec as P

HIGHEST = lax.Precision.HIGHEST
F32 = jnp.float32
BF16 = jnp.bfloat16
GROUP = 8
GRANT = 16 << 20


def cosine(length):
    rows = np.arange(length)[:, None]
    cols = np.arange(length)[None, :]
    table = np.sqrt(2.0 / length) * np.cos(np.pi * rows * (2 * cols + 1) / (2 * length))
    table[0] = math.sqrt(1.0 / length)
    return table


def eigen(length):
    return -4.0 * np.sin(np.pi * np.arange(length) / (2 * length)) ** 2


def halves(table):
    table = np.asarray(table, np.float64)
    high = table.astype(np.float32).astype(BF16)
    low = (table - high.astype(np.float64)).astype(np.float32).astype(BF16)
    return np.stack([high, low])


def sine(length):
    modes = np.arange(1, length + 1)
    return np.sqrt(2.0 / (length + 1)) * np.sin(np.pi * np.outer(modes, modes) / (length + 1))


def wall_eigen(length):
    return -4.0 * np.sin(np.pi * np.arange(1, length + 1) / (2 * (length + 1))) ** 2


def local_tables(bx, by):
    sx, sy = sine(bx), sine(by)
    along_y = np.kron(np.eye(GROUP), sy)
    along_x = np.kron(sx, np.eye(GROUP))
    faces = np.concatenate(
        [
            np.einsum("a,by->yab", sx[:, -1], sy),
            np.einsum("a,by->yab", sx[:, 0], sy),
            np.einsum("ax,b->xab", sx, sy[:, -1]),
            np.einsum("ax,b->xab", sx, sy[:, 0]),
        ]
    )
    count = faces.shape[0]
    faces = faces.reshape(count, bx, by // GROUP, GROUP).transpose(2, 0, 1, 3)
    faces = faces.reshape(by // GROUP, count, bx * GROUP)
    return along_y, along_x, faces, -faces.transpose(0, 2, 1)


def edge_rows(blocks, size):
    table = cosine(blocks * size)
    ahead = np.minimum(size * (np.arange(blocks) + 1), blocks * size - 1)
    behind = np.maximum(size * np.arange(blocks) - 1, 0)
    return table[:, ahead].T, table[:, behind].T


def phase_tables(blocks, size):
    total = blocks * size
    modes = np.arange(total)
    scale = np.where(modes == 0, math.sqrt(1.0 / total), math.sqrt(2.0 / total))
    near = np.pi * np.outer(2 * np.arange(size) + 1, modes) / (2 * total)
    far = np.pi * np.outer(np.arange(blocks), modes) * size / total
    near = np.concatenate([scale * np.cos(near), scale * np.sin(near)], 1)
    return near, np.cos(far), np.sin(far)


def split(values):
    high = values.astype(BF16)
    low = (values - high.astype(F32)).astype(BF16)
    return high, low


def dot(left, right):
    return lax.dot_general(left, right, (((1,), (0,)), ((), ())), preferred_element_type=F32)


def mm(left, right):
    return dot(
        jnp.concatenate([left[0], left[1], left[0]], 1),
        jnp.concatenate([right[0], right[0], right[1]], 0),
    )


def pair(ref, *index):
    return ref[(0, *index)], ref[(1, *index)]


def side_by_side(blocks):
    return jnp.concatenate(blocks, 1)


def iota(shape, dim):
    return lax.broadcasted_iota(jnp.int32, shape, dim)


def inverse(eig_ref, zs_ref, rows, bx, by):
    base = eig_ref[bx + rows.start : bx + rows.stop, :] - zs_ref[...]
    return [1.0 / (base + eig_ref[a : a + 1, :]) for a in range(bx)]


def first_kernel(
    gx, gy, rho_hbm, vx_hbm, vy_hbm, vz_hbm, zm_hbm, zs_hbm, eig_hbm, ay_hbm, ax_hbm, face_hbm,
    hat_ref, out_ref,
    rho_ref, vx_ref, vy_ref, vz_ref, zm_ref, zs_ref, eig_ref, ay_ref, ax_ref, face_ref,
    stage, edge, cell_sems, table_sems,
):
    bx, by, nz = vx_ref.shape
    step = 2 * GROUP
    cells = [(rho_hbm, rho_ref), (vx_hbm, vx_ref), (vy_hbm, vy_ref), (vz_hbm, vz_ref)]
    tables = [
        (zm_hbm, zm_ref), (ay_hbm, ay_ref), (ax_hbm, ax_ref),
        (eig_hbm, eig_ref), (zs_hbm, zs_ref), (face_hbm, face_ref),
    ]
    loads = []
    for part in range(bx // GROUP):
        rows = pl.ds(part * GROUP, GROUP)
        loads.append(
            [
                pltpu.make_async_copy(src.at[rows], dst.at[rows], cell_sems.at[part, i])
                for i, (src, dst) in enumerate(cells)
            ]
        )
        for load in loads[-1]:
            load.start()
        if part == 0:
            fixed = [
                pltpu.make_async_copy(src, dst, table_sems.at[i])
                for i, (src, dst) in enumerate(tables)
            ]
            for load in fixed[:2]:
                load.start()
    for load in fixed[2:]:
        load.start()

    cut_x = (lax.axis_index("gx") < gx - 1).astype(F32)
    cut_y = (lax.axis_index("gy") < gy - 1).astype(F32)
    row = iota((by, nz), 0)
    lane = iota((by, nz), 1)
    previous = None
    zm = None
    for start in range(0, bx, step):
        blocks = []
        for part in (start, start + GROUP):
            for load in loads[part // GROUP]:
                load.wait()
            layers = []
            for x in range(part, part + GROUP):
                rho = rho_ref[x].astype(F32)
                mx = rho * vx_ref[x]
                my = rho * vy_ref[x]
                mz = rho * vz_ref[x]
                total = mx if previous is None else mx - previous
                previous = mx
                below = jnp.where(row == 0, 0.0, pltpu.roll(my, 1, 0))
                total = total + (my - below)
                under = jnp.where(lane == 0, 0.0, pltpu.roll(mz, 1, 1))
                total = total + (mz - under)
                layers.append(total)
                edge[by + x : by + x + 1, :] = my[by - 1 :, :] * cut_y
                if x == bx - 1:
                    edge[0:by, :] = mx * cut_x
            if zm is None:
                fixed[0].wait()
                fixed[1].wait()
                zm = split(zm_ref[...])
            blocks.append(mm(split(jnp.concatenate(layers, 0)), zm))
        block = mm(pair(ay_ref), split(side_by_side(blocks)))
        stage[start : start + GROUP] = block[:, :nz].reshape(GROUP, by, nz)
        stage[start + GROUP : start + step] = block[:, nz:].reshape(GROUP, by, nz)
    for load in fixed[2:]:
        load.wait()
    momentum = mm(split(edge[...]), zm)
    mxs, mys = momentum[:by], momentum[by:]
    traces = jnp.concatenate([mxs, jnp.zeros_like(mxs), mys, jnp.zeros_like(mys)], 0)
    for start in range(0, by, step):
        groups = [slice(start, start + GROUP), slice(start + GROUP, start + step)]
        block = side_by_side([stage[:, rows, :].reshape(bx * GROUP, nz) for rows in groups])
        block = mm(pair(ax_ref), split(block))
        for which, rows in enumerate(groups):
            part = block[:, which * nz : (which + 1) * nz]
            hat_ref[:, rows, :] = part.reshape(bx, GROUP, nz)
            scale = jnp.concatenate(inverse(eig_ref, zs_ref, rows, bx, by), 0)
            traces = traces + mm(pair(face_ref, rows.start // GROUP), split(part * scale))
    turned = traces.T
    each = out_ref.shape[1]
    for peer in range(out_ref.shape[0]):
        out_ref[peer] = turned[peer * each : (peer + 1) * each, :]


def middle_kernel(
    gx, gy, bx, by, in_ref, zs_ref, eig_ref, nx_ref, ny_ref, nxt_ref, nyt_ref,
    far_x_ref, far_y_ref, uxt_ref, uy_ref, ux_ref, uyt_ref, out_ref,
):
    peers, each, lanes = in_ref.shape
    me = lax.axis_index("gx") * gy + lax.axis_index("gy")
    total_x, total_y = gx * bx, gy * by
    nz = peers * each
    blocks = [in_ref[:, c, :] for c in range(each)]
    data = jnp.concatenate(blocks, 0)
    turned = data.T

    near = []
    for part in pair(nx_ref):
        none = jnp.zeros_like(part)
        rest = jnp.zeros((2 * bx, 2 * part.shape[1]), BF16)
        near.append(
            jnp.concatenate([side_by_side([part, none]), side_by_side([none, part]), rest], 0)
        )
    wave = mm(split(data), near)
    far_xc, far_xs = far_x_ref[0], far_x_ref[1]
    sides = []
    for face in range(2):
        base = 2 * total_y * face
        row_blocks = []
        for c in range(each):
            rows = slice(c * peers, (c + 1) * peers)
            cosine_part = wave[rows, base : base + total_y]
            sine_part = wave[rows, base + total_y : base + 2 * total_y]
            row_blocks.append(cosine_part * far_xc - sine_part * far_xs)
        sides.append(side_by_side(row_blocks))
    from_x = split(jnp.concatenate(sides, 0))

    first = 2 * by
    faces = side_by_side([turned[first : first + bx], turned[first + bx :]])
    wave = mm(pair(ny_ref), split(faces))
    far_yc = side_by_side([far_y_ref[0], far_y_ref[0]])
    far_ys = side_by_side([far_y_ref[1], far_y_ref[1]])
    from_y = split(wave[:total_x] * far_yc - wave[total_x:] * far_ys)

    spread = []
    for part in pair(uy_ref):
        none = jnp.zeros((peers, total_y), BF16)
        rows = []
        for face in range(2):
            values = part[face * peers : (face + 1) * peers]
            for c in range(each):
                rows.append(side_by_side([values if c == k else none for k in range(each)]))
        spread.append(jnp.concatenate(rows, 0))
    uxt = pair(uxt_ref)
    spectrum = dot(
        side_by_side([from_y[0], from_y[1], from_y[0], uxt[0], uxt[0], uxt[1]]),
        jnp.concatenate(
            [spread[0], spread[0], spread[1], from_x[0], from_x[1], from_x[0]], 0
        ),
    )
    solved = []
    for c in range(each):
        divisor = eig_ref[...] - zs_ref[me * each + c]
        solved.append(split(spectrum[:, c * total_y : (c + 1) * total_y] / divisor))
    high = side_by_side([part[0] for part in solved])
    low = side_by_side([part[1] for part in solved])

    along = mm(pair(ux_ref), (high, low))
    rows = []
    for c in range(each):
        columns = slice(c * total_y, (c + 1) * total_y)
        upper, lower = along[:peers, columns], along[peers:, columns]
        rows.append(side_by_side([upper * far_xc, -upper * far_xs, lower * far_xc, -lower * far_xs]))
    back = mm(split(jnp.concatenate(rows, 0)), pair(nxt_ref))

    lane = iota((total_x, 2 * nz), 1)
    owner = (lane % nz) // peers
    uyt = pair(uyt_ref)
    along = None
    for c in range(each):
        part = mm(solved[c], uyt)
        along = part if along is None else jnp.where(owner == c, part, along)
    wave = split(jnp.concatenate([along * far_yc, -along * far_ys], 0))
    wave = mm(pair(nyt_ref), wave)
    other = jnp.concatenate([jnp.zeros((2 * by, nz), F32), wave[:, :nz], wave[:, nz:]], 0)
    back = back + other.T

    row = iota((peers, lanes), 0)
    lane = iota((peers, lanes), 1)
    row_x, row_y = row // gy, row % gy
    face = jnp.where(lane < by, 0, jnp.where(lane < 2 * by, 1, jnp.where(lane < 2 * by + bx, 2, 3)))
    coord = jnp.where(face < 2, row_x, row_y)
    end = jnp.where(face < 2, gx - 1, gy - 1)
    cut = jnp.where(face % 2 == 0, end - coord, coord) > 0
    for c in range(each):
        block = blocks[c]
        ahead, behind = pltpu.roll(block, lanes - by, 1), pltpu.roll(block, by, 1)
        ahead_x, behind_x = pltpu.roll(ahead, peers - gy, 0), pltpu.roll(behind, gy, 0)
        if bx != by:
            ahead, behind = pltpu.roll(block, lanes - bx, 1), pltpu.roll(block, bx, 1)
        ahead_y, behind_y = pltpu.roll(ahead, peers - 1, 0), pltpu.roll(behind, 1, 0)
        across = jnp.where(
            face == 0, ahead_x,
            jnp.where(face == 1, behind_x, jnp.where(face == 2, ahead_y, behind_y)),
        )
        across = jnp.where(cut, across, block)
        out_ref[:, c, :] = across - back[c * peers : (c + 1) * peers]


def last_kernel(
    gx, gy, flux_ref, hat_ref, rho_ref, vx_ref, vy_ref, vz_ref, zm_ref, zs_ref, eig_ref,
    ay_ref, ax_ref, back_ref, ox_hbm, oy_hbm, oz_hbm, ox_ref, oy_ref, oz_ref, stage, sems,
):
    bx, by, nz = vx_ref.shape
    step = 2 * GROUP
    last_x = lax.axis_index("gx") == gx - 1
    last_y = lax.axis_index("gy") == gy - 1
    zt = split(zm_ref[...].T)
    flux = jnp.concatenate([flux_ref[peer] for peer in range(flux_ref.shape[0])], 0).T
    flux_parts = split(flux)
    for start in range(0, by, step):
        blocks = []
        for rows in (slice(start, start + GROUP), slice(start + GROUP, start + step)):
            block = hat_ref[:, rows, :].reshape(bx * GROUP, nz)
            block = block + mm(pair(back_ref, rows.start // GROUP), flux_parts)
            blocks.append(block * jnp.concatenate(inverse(eig_ref, zs_ref, rows, bx, by), 0))
        block = mm(pair(ax_ref), split(side_by_side(blocks)))
        stage[:, start : start + GROUP, :] = block[:, :nz].reshape(bx, GROUP, nz)
        stage[:, start + GROUP : start + step, :] = block[:, nz:].reshape(bx, GROUP, nz)
    edges = mm(split(jnp.concatenate([flux[:by], flux[2 * by : 2 * by + bx]], 0)), zt)
    row = iota((by, nz), 0)
    lane = iota((by, nz), 1)
    layers = []
    stores = []
    done = 0
    for start in range(0, bx, step):
        parts = (slice(start, start + GROUP), slice(start + GROUP, start + step))
        block = side_by_side([stage[part].reshape(GROUP * by, nz) for part in parts])
        block = mm(pair(ay_ref), split(block))
        for which in range(2):
            values = mm(split(block[:, which * nz : (which + 1) * nz]), zt)
            layers += [values[i * by : (i + 1) * by] for i in range(GROUP)]
        ready = len(layers) if len(layers) == bx else len(layers) - GROUP
        for x in range(done, ready):
            here = layers[x]
            rho = 1.0 / rho_ref[x].astype(F32)
            if x < bx - 1:
                following = layers[x + 1]
            else:
                following = jnp.where(last_x, 0.0, edges[:by])
            ox_ref[x] = vx_ref[x] - (following - here) * rho
            cut = jnp.broadcast_to(edges[by + x : by + x + 1, :], (by, nz))
            cut = jnp.where(last_y, 0.0, cut)
            following = jnp.where(row == by - 1, cut, pltpu.roll(here, by - 1, 0))
            oy_ref[x] = vy_ref[x] - (following - here) * rho
            following = jnp.where(lane == nz - 1, 0.0, pltpu.roll(here, nz - 1, 1))
            oz_ref[x] = vz_ref[x] - (following - here) * rho
            if (x + 1) % GROUP == 0:
                part = x // GROUP
                rows = pl.ds(part * GROUP, GROUP)
                for i, (src, dst) in enumerate(
                    [(ox_ref, ox_hbm), (oy_ref, oy_hbm), (oz_ref, oz_hbm)]
                ):
                    store = pltpu.make_async_copy(src.at[rows], dst.at[rows], sems.at[part, i])
                    store.start()
                    stores.append(store)
        done = ready
    for store in stores:
        store.wait()


def call(kernel, outs, scratch, args, spaces=None, out_space=pltpu.VMEM):
    spaces = spaces or {}
    specs = [
        pl.BlockSpec(memory_space=spaces.get(i, spaces.get("rest", pltpu.VMEM)))
        for i in range(len(args))
    ]
    return pl.pallas_call(
        kernel,
        out_shape=[jax.ShapeDtypeStruct(shape, F32) for shape in outs],
        in_specs=specs,
        out_specs=[pl.BlockSpec(memory_space=out_space)] * len(outs),
        scratch_shapes=scratch,
        compiler_params=pltpu.CompilerParams(vmem_limit_bytes=GRANT),
    )(*args)


def by_faces(density, vel_x, vel_y, vel_z, z_modes, z_stiffness):
    bx, by, nz = vel_x.shape
    gx, gy = lax.axis_size("gx"), lax.axis_size("gy")
    peers = gx * gy
    each = nz // peers
    lanes = 2 * (bx + by)
    along_y, along_x, faces, back = (halves(table) for table in local_tables(bx, by))
    f32 = lambda table: np.asarray(table, np.float32)
    eig = np.concatenate([wall_eigen(bx), wall_eigen(by)])[:, None]
    eig = f32(np.broadcast_to(eig, (bx + by, nz)))
    stiff = z_stiffness.reshape(1, nz)
    args = (density, vel_x, vel_y, vel_z, z_modes, stiff, eig, along_y, along_x, faces)
    args = [pltpu.with_memory_space_constraint(jnp.asarray(arg), pltpu.HBM) for arg in args]
    hat, sent = call(
        functools.partial(first_kernel, gx, gy),
        [(bx, by, nz), (peers, each, lanes)],
        [pltpu.VMEM(arg.shape, arg.dtype) for arg in args]
        + [
            pltpu.VMEM((bx, by, nz), F32),
            pltpu.VMEM((bx + by, nz), F32),
            pltpu.SemaphoreType.DMA((bx // GROUP, 4)),
            pltpu.SemaphoreType.DMA((6,)),
        ],
        args,
        {"rest": pltpu.HBM},
    )
    got = lax.all_to_all(sent, ("gx", "gy"), 0, 0, tiled=True)

    near_x, cos_x, sin_x = phase_tables(gy, by)
    near_y, cos_y, sin_y = phase_tables(gx, bx)
    row_x, row_y = np.arange(peers) // gy, np.arange(peers) % gy
    far_x = f32(np.stack([cos_x[row_y], sin_x[row_y]]))
    far_y = np.stack([np.tile(table[row_x], (each, 1)).T for table in (cos_y, sin_y)])
    ahead_x, behind_x = edge_rows(gx, bx)
    ahead_y, behind_y = edge_rows(gy, by)
    ux = np.concatenate([ahead_x[row_x], behind_x[row_x]], 0)
    uy = np.concatenate([ahead_y[row_y], behind_y[row_y]], 0)
    uyt = np.concatenate([np.tile(table[row_y], (each, 1)).T for table in (ahead_y, behind_y)], 1)
    total_x, total_y = gx * bx, gy * by
    nxt = np.zeros((2, 2 * total_y, lanes))
    for face in range(2):
        nxt[face, :, face * by : (face + 1) * by] = near_x.T
    nxt = nxt.reshape(4 * total_y, lanes)
    (solved,) = call(
        functools.partial(middle_kernel, gx, gy, bx, by),
        [(peers, each, lanes)],
        [],
        (got, z_stiffness, f32(eigen(total_x)[:, None] + eigen(total_y)[None, :]),
         halves(near_x), halves(near_y.T), halves(nxt), halves(near_y),
         far_x, f32(far_y), halves(ux.T), halves(uy), halves(ux), halves(uyt)),
        {1: pltpu.SMEM},
    )
    flux = lax.all_to_all(solved, ("gx", "gy"), 0, 0, tiled=True)
    block = pltpu.VMEM((bx, by, nz), F32)
    return call(
        functools.partial(last_kernel, gx, gy),
        [(bx, by, nz)] * 3,
        [block] * 4 + [pltpu.SemaphoreType.DMA((bx // GROUP, 3))],
        (flux, hat, density, vel_x, vel_y, vel_z, z_modes, stiff, eig, along_y, along_x, back),
        None,
        pltpu.HBM,
    )


def from_behind(block, axis, distance):
    devices = range(lax.axis_size(axis))
    route = [(i - distance, i) for i in devices if i - distance in devices]
    return lax.ppermute(block, axis, route)


def cosine_table(length):
    rows = lax.broadcasted_iota(jnp.int32, (length, length), 0)
    cols = lax.broadcasted_iota(jnp.int32, (length, length), 1)
    phase = rows * (2 * cols + 1) % (4 * length)
    angle = phase.astype(jnp.float32) * (math.pi / (2 * length))
    scales = jnp.where(rows == 0, math.sqrt(1.0 / length), math.sqrt(2.0 / length))
    return scales * jnp.cos(angle)


def upper_step(values):
    padding = [(0, 0)] * (values.ndim - 1) + [(0, 1)]
    return jnp.pad(values[..., 1:], padding) - values


def lower_step(values):
    padding = [(0, 0)] * (values.ndim - 1) + [(1, 0)]
    return values - jnp.pad(values[..., :-1], padding)


def eigenvalues(modes, length):
    return -(2.0 - 2.0 * jnp.cos(jnp.pi * modes / length))


def by_transposes(density, vel_x, vel_y, vel_z, z_modes, z_stiffness):
    cells_x = vel_x.shape[0]
    cells_y = vel_x.shape[1]
    depth = vel_x.shape[2]
    groups_x = lax.axis_size("gx")
    groups_y = lax.axis_size("gy")
    total_x = cells_x * groups_x
    total_y = cells_y * groups_y
    planes_dev = depth // groups_x
    xmodes_dev = total_x // groups_y
    table_x = cosine_table(total_x)
    table_y = cosine_table(total_y)
    heaviness = density.astype(jnp.float32)
    momentum_x = heaviness * vel_x
    momentum_y = heaviness * vel_y
    momentum_z = heaviness * vel_z
    below_x = from_behind(momentum_x[cells_x - 1 :], "gx", 1)
    below_y = from_behind(momentum_y[:, cells_y - 1 :], "gy", 1)
    diff_x = momentum_x - jnp.concatenate([below_x, momentum_x[:-1]], 0)
    diff_y = momentum_y - jnp.concatenate([below_y, momentum_y[:, :-1]], 1)
    source = diff_x + diff_y + lower_step(momentum_z)
    vertical = jnp.dot(source.reshape(cells_x * cells_y, depth), z_modes, precision=HIGHEST)
    vertical = vertical.reshape(cells_x, cells_y, groups_x, planes_dev).transpose(0, 2, 1, 3)
    vertical = vertical.reshape(cells_x, groups_x, cells_y * planes_dev)
    lines_x = lax.all_to_all(vertical, "gx", split_axis=1, concat_axis=0, tiled=True)
    lines_x = lines_x.reshape(total_x, cells_y, planes_dev)
    mixed = jnp.einsum("xyk,ax->yak", lines_x, table_x, precision=HIGHEST)
    mixed = mixed.reshape(cells_y, groups_y, xmodes_dev * planes_dev)
    lines_y = lax.all_to_all(mixed, "gy", split_axis=1, concat_axis=0, tiled=True)
    right_side = lines_y.reshape(total_y, xmodes_dev * planes_dev)
    spectrum = jnp.dot(table_y, right_side, precision=HIGHEST)
    z_first = lax.axis_index("gx") * planes_dev
    stiff_dev = lax.dynamic_slice_in_dim(z_stiffness, z_first, planes_dev)
    x_first = lax.axis_index("gy") * xmodes_dev
    modes_x = (x_first + jnp.arange(xmodes_dev, dtype=jnp.int32)).astype(jnp.float32)
    modes_y = jnp.arange(total_y, dtype=jnp.int32).astype(jnp.float32)
    divisor = (
        eigenvalues(modes_x, total_x)[None, :, None]
        + eigenvalues(modes_y, total_y)[:, None, None]
        - stiff_dev[None, None, :]
    )
    pressure_hat = spectrum / divisor.reshape(total_y, xmodes_dev * planes_dev)
    y_space = jnp.einsum("by,bc->yc", table_y, pressure_hat, precision=HIGHEST)
    modes_split = z_modes.reshape(depth, groups_x, planes_dev)
    sent_y = y_space.reshape(total_y, 1, xmodes_dev * planes_dev)
    lines_back = lax.all_to_all(sent_y, "gy", split_axis=0, concat_axis=1, tiled=True)
    lines_back = lines_back.reshape(cells_y, total_x, planes_dev)
    space_x = jnp.einsum("yak,ax->xyk", lines_back, table_x, precision=HIGHEST)
    sent_x = space_x.reshape(total_x, 1, cells_y * planes_dev)
    blocks = lax.all_to_all(sent_x, "gx", split_axis=0, concat_axis=1, tiled=True)
    blocks = blocks.reshape(cells_x, groups_x, cells_y, planes_dev)
    pressure = jnp.einsum("xhyk,zhk->xyz", blocks, modes_split, precision=HIGHEST)
    rim_x = from_behind(pressure[0:1], "gx", -1)
    grad_x = jnp.concatenate([pressure[1:], rim_x], 0) - pressure
    rim_y = from_behind(pressure[:, 0:1], "gy", -1)
    grad_y = jnp.concatenate([pressure[:, 1:], rim_y], 1) - pressure
    grad_z = upper_step(pressure)
    new_x = vel_x - grad_x / heaviness
    new_y = vel_y - grad_y / heaviness
    new_z = vel_z - grad_z / heaviness
    return (new_x, new_y, new_z)


def solution(mesh):
    sizes = mesh.shape
    peers = sizes["gx"] * sizes["gy"]

    def local(density, vel_x, vel_y, vel_z, z_modes, z_stiffness):
        cells_x, cells_y, depth = vel_x.shape
        fits = depth % peers == 0 and depth % 128 == 0
        fits = fits and cells_x % (2 * GROUP) == 0 and cells_y % (2 * GROUP) == 0
        fits = fits and 2 * (cells_x + cells_y) % 128 == 0
        plan = by_faces if fits else by_transposes
        return tuple(plan(density, vel_x, vel_y, vel_z, z_modes, z_stiffness))

    block = P("gx", "gy", None)
    return jax.shard_map(
        local,
        mesh=mesh,
        in_specs=(block, block, block, block, P(), P()),
        out_specs=(block, block, block),
        check_vma=False,
    )
```

```python
import functools
import math

import jax
import jax.numpy as jnp
import numpy as np
from jax import lax
from jax.experimental import pallas as pl
from jax.experimental.pallas import tpu as pltpu
from jax.sharding import PartitionSpec as P

HIGHEST = lax.Precision.HIGHEST
F32 = jnp.float32
BF16 = jnp.bfloat16
GROUP = 8
GRANT = 16 << 20
LOADS = 1
FACTORS = ("rows_x", "rows_y", "faces_x", "faces_y")


def cosine(length):
    rows = np.arange(length)[:, None]
    cols = np.arange(length)[None, :]
    table = np.sqrt(2.0 / length) * np.cos(np.pi * rows * (2 * cols + 1) / (2 * length))
    table[0] = math.sqrt(1.0 / length)
    return table


def eigen(length):
    return -4.0 * np.sin(np.pi * np.arange(length) / (2 * length)) ** 2


def halves(table):
    table = np.asarray(table, np.float64)
    high = table.astype(np.float32).astype(BF16)
    low = (table - high.astype(np.float64)).astype(np.float32).astype(BF16)
    return np.stack([high, low])


def sine(length):
    modes = np.arange(1, length + 1)
    return np.sqrt(2.0 / (length + 1)) * np.sin(np.pi * np.outer(modes, modes) / (length + 1))


def wall_eigen(length):
    return -4.0 * np.sin(np.pi * np.arange(1, length + 1) / (2 * (length + 1))) ** 2


def local_tables(bx, by):
    sx, sy = sine(bx), sine(by)
    rows_x = np.repeat(sx, GROUP, 1)
    rows_y = np.tile(sy, (1, GROUP))
    faces_x = np.concatenate(
        [np.tile(sx[:, -1:], (1, by)), np.tile(sx[:, :1], (1, by)), sx, sx], 1
    )
    faces_y = np.concatenate(
        [sy, sy, np.tile(sy[:, -1:], (1, bx)), np.tile(sy[:, :1], (1, bx))], 1
    )
    return rows_x, rows_y, faces_x, faces_y


def edge_rows(blocks, size):
    table = cosine(blocks * size)
    ahead = np.minimum(size * (np.arange(blocks) + 1), blocks * size - 1)
    behind = np.maximum(size * np.arange(blocks) - 1, 0)
    return table[:, ahead].T, table[:, behind].T


def phase_tables(blocks, size):
    total = blocks * size
    modes = np.arange(total)
    scale = np.where(modes == 0, math.sqrt(1.0 / total), math.sqrt(2.0 / total))
    near = np.pi * np.outer(2 * np.arange(size) + 1, modes) / (2 * total)
    far = np.pi * np.outer(np.arange(blocks), modes) * size / total
    near = np.concatenate([scale * np.cos(near), scale * np.sin(near)], 1)
    return near, np.cos(far), np.sin(far)


class Pack:
    def __init__(self, kind):
        self.kind, self.rows, self.parts, self.places = kind, 0, [], {}

    def add(self, name, table):
        height, width = table.shape
        wide = -(-width // 128) * 128
        table = np.pad(np.asarray(table), ((0, 0), (0, wide - width)))
        self.places[name] = (self.rows, height, wide // 128)
        for first in range(0, wide, 128):
            self.parts.append(table[:, first : first + 128].astype(self.kind))
            self.rows += height
        assert height % 16 == 0

    def array(self):
        return jnp.asarray(np.concatenate(self.parts, 0))

    def read(self, ref, name):
        first, height, count = self.places[name]
        parts = [ref[first + i * height : first + (i + 1) * height, :] for i in range(count)]
        return parts[0] if count == 1 else jnp.concatenate(parts, 1)


def stack_pair(pack, name, table):
    high, low = halves(table)
    pack.add(name + "_high", high)
    pack.add(name + "_low", low)


def split(values):
    high = values.astype(BF16)
    low = (values - high.astype(F32)).astype(BF16)
    return high, low


def dot(left, right):
    return lax.dot_general(left, right, (((1,), (0,)), ((), ())), preferred_element_type=F32)


def mm(left, right):
    return dot(
        jnp.concatenate([left[0], left[1], left[0]], 1),
        jnp.concatenate([right[0], right[0], right[1]], 0),
    )


def pair(ref, *index):
    return ref[(0, *index)], ref[(1, *index)]


def side_by_side(blocks):
    return jnp.concatenate(blocks, 1)


def iota(shape, dim):
    return lax.broadcasted_iota(jnp.int32, shape, dim)


def build_tables(rows_x, rows_y, faces_x, faces_y, ay_ref, ax_ref, back_ref, face_ref):
    bx, by = rows_x.shape[0], rows_y.shape[0]

    def halves_of(values):
        high = values.astype(BF16).astype(F32)
        return high, values - high

    for which, values in enumerate(halves_of(rows_y)):
        lane = iota(values.shape, 1)
        for k in range(GROUP):
            rows = slice(k * by, (k + 1) * by)
            ay_ref[which, rows, :] = jnp.where(lane // by == k, values, 0.0).astype(BF16)
    for which, values in enumerate(halves_of(rows_x)):
        shape = (GROUP, values.shape[1])
        same = iota(shape, 1) % GROUP == iota(shape, 0)
        for a in range(0, bx, 2):
            rows = [
                jnp.where(same, jnp.broadcast_to(values[i : i + 1, :], shape), 0.0)
                for i in (a, a + 1)
            ]
            rows = jnp.concatenate(rows, 0).astype(BF16)
            ax_ref[which, a * GROUP : (a + 2) * GROUP, :] = rows
    for group in range(by // GROUP):
        along = faces_y[group * GROUP : (group + 1) * GROUP, :]
        rows = jnp.concatenate([along * faces_x[a : a + 1, :] for a in range(bx)], 0)
        for which, part in enumerate(split(-rows)):
            back_ref[which, group] = part
        for which, part in enumerate(split(rows.T)):
            face_ref[which, group] = part


def first_kernel(
    gx, gy, pack, parts, count, *refs,
):
    hbm, refs = refs[:count], refs[count:]
    hat_ref, out_ref, scale_ref, own_ref, ay_ref, ax_ref, back_ref = refs[:7]
    kept, refs = refs[7 : 7 + count], refs[7 + count :]
    stage, edge, face_ref, cell_sems, table_sems = refs
    rho_ref, vx_ref, vy_ref, vz_ref, own_tables, zs_ref, zm_ref = kept[:7]
    bx, by, nz = vx_ref.shape
    step = 2 * GROUP
    size = bx // parts
    loads = []
    for part in range(parts):
        rows = pl.ds(part * size, size)
        loads.append(
            [
                pltpu.make_async_copy(hbm[i].at[rows], kept[i].at[rows], cell_sems.at[part, i])
                for i in range(4)
            ]
        )
    tables = {
        i: pltpu.make_async_copy(hbm[i], kept[i], table_sems.at[i - 4]) for i in range(4, count)
    }
    order = [tables[4], tables[5], *loads[0], tables[6]]
    for more in loads[1:]:
        order += more
    for load in order:
        load.start()

    cut_x = (lax.axis_index("gx") < gx - 1).astype(F32)
    cut_y = (lax.axis_index("gy") < gy - 1).astype(F32)
    row = iota((by, nz), 0)
    lane = iota((by, nz), 1)

    tables[4].wait()
    tables[5].wait()
    me = lax.axis_index("gx") * gy + lax.axis_index("gy")
    each = out_ref.shape[1]
    for c in range(each):
        mine = jnp.where(iota((1, nz), 1) == me * each + c, zs_ref[...], 0.0)
        mine = jnp.sum(mine, 1, keepdims=True)
        own_ref[c : c + 1, :] = jnp.broadcast_to(mine, (1, own_ref.shape[1]))
    eig_x, eig_y = pack.read(own_tables, "eig_x"), pack.read(own_tables, "eig_y")
    for a in range(bx):
        scale_ref[a] = 1.0 / (eig_y - zs_ref[...] + eig_x[a : a + 1, :])
    factors = [pack.read(own_tables, name) for name in FACTORS]
    build_tables(*factors, ay_ref, ax_ref, back_ref, face_ref)

    def source(start, previous):
        layers = []
        for x in range(start, start + GROUP):
            rho = rho_ref[x].astype(F32)
            mx = rho * vx_ref[x]
            my = rho * vy_ref[x]
            mz = rho * vz_ref[x]
            total = mx if previous is None else mx - previous
            previous = mx
            below = jnp.where(row == 0, 0.0, pltpu.roll(my, 1, 0))
            total = total + (my - below)
            under = jnp.where(lane == 0, 0.0, pltpu.roll(mz, 1, 1))
            total = total + (mz - under)
            layers.append(total)
            edge[by + x : by + x + 1, :] = my[by - 1 :, :] * cut_y
            if x == bx - 1:
                edge[0:by, :] = mx * cut_x
        return split(jnp.concatenate(layers, 0)), previous

    previous = None
    zm = None
    lines = []
    for start in range(0, bx, step):
        if start % size == 0:
            for load in loads[start // size]:
                load.wait()
            if start // size == parts - 1:
                for i in range(7, count):
                    tables[i].start()
            if zm is None:
                tables[6].wait()
                zm = split(zm_ref[...])
        lines = []
        for first in (start, start + GROUP):
            values, previous = source(first, previous)
            lines.append(mm(values, zm))
        block = mm((ay_ref[0], ay_ref[1]), split(side_by_side(lines)))
        stage[start : start + GROUP] = block[:, :nz].reshape(GROUP, by, nz)
        stage[start + GROUP : start + step] = block[:, nz:].reshape(GROUP, by, nz)
    momentum = mm(split(edge[...]), zm)
    mxs, mys = momentum[:by], momentum[by:]
    traces = jnp.concatenate([mxs, jnp.zeros_like(mxs), mys, jnp.zeros_like(mys)], 0)
    for start in range(0, by, step):
        groups = [slice(start, start + GROUP), slice(start + GROUP, start + step)]
        block = side_by_side([stage[:, rows, :].reshape(bx * GROUP, nz) for rows in groups])
        block = mm(pair(ax_ref), split(block))
        for which, rows in enumerate(groups):
            part = block[:, which * nz : (which + 1) * nz]
            hat_ref[:, rows, :] = part.reshape(bx, GROUP, nz)
            part = part * scale_ref[:, rows, :].reshape(bx * GROUP, nz)
            traces = traces + mm(pair(face_ref, rows.start // GROUP), split(part))
    turned = traces.T
    for peer in range(out_ref.shape[0]):
        out_ref[peer] = turned[peer * each : (peer + 1) * each, :]
    for i in range(7, count):
        tables[i].wait()


def middle_kernel(
    gx, gy, bx, by, narrow_pack, full_pack, in_ref, own_ref, narrow_ref, full_ref, out_ref,
):
    peers, each, lanes = in_ref.shape
    total_x, total_y = gx * bx, gy * by
    nz = peers * each
    blocks = [in_ref[:, c, :] for c in range(each)]
    data = jnp.concatenate(blocks, 0)
    turned = data.T

    def narrow(name):
        return narrow_pack.read(narrow_ref, name)

    def narrow_pair(name):
        return narrow(name + "_high"), narrow(name + "_low")

    def full(name):
        return full_pack.read(full_ref, name)

    near = []
    for part in narrow_pair("nx"):
        none = jnp.zeros_like(part)
        rest = jnp.zeros((2 * bx, 2 * part.shape[1]), BF16)
        near.append(
            jnp.concatenate([side_by_side([part, none]), side_by_side([none, part]), rest], 0)
        )
    wave = mm(split(data), near)
    far_xc, far_xs = full("far_xc"), full("far_xs")
    sides = []
    for face in range(2):
        base = 2 * total_y * face
        row_blocks = []
        for c in range(each):
            rows = slice(c * peers, (c + 1) * peers)
            cosine_part = wave[rows, base : base + total_y]
            sine_part = wave[rows, base + total_y : base + 2 * total_y]
            row_blocks.append(cosine_part * far_xc - sine_part * far_xs)
        sides.append(side_by_side(row_blocks))
    from_x = split(jnp.concatenate(sides, 0))

    first = 2 * by
    faces = side_by_side([turned[first : first + bx], turned[first + bx :]])
    high, low = split(faces)
    wave = dot(
        narrow("ny_stack"),
        jnp.concatenate([high, low, high, jnp.zeros((128 - 3 * bx, 2 * nz), BF16)], 0),
    )
    far_yc = side_by_side([full("far_yc")] * 2)
    far_ys = side_by_side([full("far_ys")] * 2)
    from_y = split(wave[:total_x] * far_yc - wave[total_x:] * far_ys)

    spread = []
    for part in narrow_pair("uy"):
        none = jnp.zeros((peers, total_y), BF16)
        rows = []
        for face in range(2):
            values = part[face * peers : (face + 1) * peers]
            for c in range(each):
                rows.append(side_by_side([values if c == k else none for k in range(each)]))
        spread.append(jnp.concatenate(rows, 0))
    uxt = narrow("uxt")
    spectrum = dot(
        side_by_side([from_y[0], from_y[1], from_y[0], uxt, uxt[:, : 2 * peers]]),
        jnp.concatenate(
            [spread[0], spread[0], spread[1], from_x[0], from_x[0], from_x[1]], 0
        ),
    )
    solved = []
    for c in range(each):
        divisor = full("eig") - own_ref[c : c + 1, :]
        solved.append(split(spectrum[:, c * total_y : (c + 1) * total_y] / divisor))
    high = side_by_side([part[0] for part in solved])
    low = side_by_side([part[1] for part in solved])

    along = mm(narrow_pair("ux"), (high, low))
    rows = []
    for c in range(each):
        columns = slice(c * total_y, (c + 1) * total_y)
        upper, lower = along[:peers, columns], along[peers:, columns]
        rows.append(side_by_side([upper * far_xc, -upper * far_xs, lower * far_xc, -lower * far_xs]))
    back = mm(split(jnp.concatenate(rows, 0)), narrow_pair("nxt"))

    lane = iota((total_x, 2 * nz), 1)
    owner = (lane % nz) // peers
    uyt = narrow_pair("uyt")
    along = None
    for c in range(each):
        part = mm(solved[c], uyt)
        along = part if along is None else jnp.where(owner == c, part, along)
    wave = split(jnp.concatenate([along * far_yc, -along * far_ys], 0))
    wave = mm(narrow_pair("nyt"), wave)
    other = jnp.concatenate([jnp.zeros((2 * by, nz), F32), wave[:, :nz], wave[:, nz:]], 0)
    back = back + other.T

    row = iota((peers, lanes), 0)
    lane = iota((peers, lanes), 1)
    row_x, row_y = row // gy, row % gy
    face = jnp.where(lane < by, 0, jnp.where(lane < 2 * by, 1, jnp.where(lane < 2 * by + bx, 2, 3)))
    coord = jnp.where(face < 2, row_x, row_y)
    end = jnp.where(face < 2, gx - 1, gy - 1)
    cut = jnp.where(face % 2 == 0, end - coord, coord) > 0
    for c in range(each):
        block = blocks[c]
        ahead, behind = pltpu.roll(block, lanes - by, 1), pltpu.roll(block, by, 1)
        ahead_x, behind_x = pltpu.roll(ahead, peers - gy, 0), pltpu.roll(behind, gy, 0)
        if bx != by:
            ahead, behind = pltpu.roll(block, lanes - bx, 1), pltpu.roll(block, bx, 1)
        ahead_y, behind_y = pltpu.roll(ahead, peers - 1, 0), pltpu.roll(behind, 1, 0)
        across = jnp.where(
            face == 0, ahead_x,
            jnp.where(face == 1, behind_x, jnp.where(face == 2, ahead_y, behind_y)),
        )
        across = jnp.where(cut, across, block)
        out_ref[:, c, :] = across - back[c * peers : (c + 1) * peers]


def last_kernel(
    gx, gy, flux_ref, hat_ref, scale_ref, rho_ref, vx_ref, vy_ref, vz_ref, zm_ref,
    ay_ref, ax_ref, back_ref, ox_hbm, oy_hbm, oz_hbm, ox_ref, oy_ref, oz_ref, stage, sems,
):
    bx, by, nz = vx_ref.shape
    step = 2 * GROUP
    last_x = lax.axis_index("gx") == gx - 1
    last_y = lax.axis_index("gy") == gy - 1
    zt = split(zm_ref[...].T)
    flux = jnp.concatenate([flux_ref[peer] for peer in range(flux_ref.shape[0])], 0).T
    flux_parts = split(flux)
    for start in range(0, by, step):
        blocks = []
        for rows in (slice(start, start + GROUP), slice(start + GROUP, start + step)):
            block = hat_ref[:, rows, :].reshape(bx * GROUP, nz)
            block = block + mm(pair(back_ref, rows.start // GROUP), flux_parts)
            blocks.append(block * scale_ref[:, rows, :].reshape(bx * GROUP, nz))
        block = mm(pair(ax_ref), split(side_by_side(blocks)))
        stage[:, start : start + GROUP, :] = block[:, :nz].reshape(bx, GROUP, nz)
        stage[:, start + GROUP : start + step, :] = block[:, nz:].reshape(bx, GROUP, nz)
    edges = mm(split(jnp.concatenate([flux[:by], flux[2 * by : 2 * by + bx]], 0)), zt)
    row = iota((by, nz), 0)
    lane = iota((by, nz), 1)
    layers = []
    stores = []
    done = 0
    for start in range(0, bx, step):
        parts = (slice(start, start + GROUP), slice(start + GROUP, start + step))
        block = side_by_side([stage[part].reshape(GROUP * by, nz) for part in parts])
        block = mm(pair(ay_ref), split(block))
        for which in range(2):
            values = mm(split(block[:, which * nz : (which + 1) * nz]), zt)
            layers += [values[i * by : (i + 1) * by] for i in range(GROUP)]
        ready = len(layers) if len(layers) == bx else len(layers) - GROUP
        for x in range(done, ready):
            here = layers[x]
            rho = 1.0 / rho_ref[x].astype(F32)
            if x < bx - 1:
                following = layers[x + 1]
            else:
                following = jnp.where(last_x, 0.0, edges[:by])
            ox_ref[x] = vx_ref[x] - (following - here) * rho
            cut = jnp.broadcast_to(edges[by + x : by + x + 1, :], (by, nz))
            cut = jnp.where(last_y, 0.0, cut)
            following = jnp.where(row == by - 1, cut, pltpu.roll(here, by - 1, 0))
            oy_ref[x] = vy_ref[x] - (following - here) * rho
            following = jnp.where(lane == nz - 1, 0.0, pltpu.roll(here, nz - 1, 1))
            oz_ref[x] = vz_ref[x] - (following - here) * rho
            if (x + 1) % GROUP == 0:
                part = x // GROUP
                rows = pl.ds(part * GROUP, GROUP)
                for i, (src, dst) in enumerate(
                    [(ox_ref, ox_hbm), (oy_ref, oy_hbm), (oz_ref, oz_hbm)]
                ):
                    store = pltpu.make_async_copy(src.at[rows], dst.at[rows], sems.at[part, i])
                    store.start()
                    stores.append(store)
        done = ready
    for store in stores:
        store.wait()


def call(kernel, outs, scratch, args, in_space=pltpu.VMEM, out_space=pltpu.VMEM):
    placed = [pltpu.with_memory_space_constraint(arg, in_space) for arg in args]
    return pl.pallas_call(
        kernel,
        out_shape=[out_space(shape, dtype) for shape, dtype in outs],
        in_specs=[pl.BlockSpec(memory_space=in_space)] * len(args),
        out_specs=[pl.BlockSpec(memory_space=out_space)] * len(outs),
        scratch_shapes=scratch,
        compiler_params=pltpu.CompilerParams(vmem_limit_bytes=GRANT),
    )(*placed)


def by_faces(density, vel_x, vel_y, vel_z, z_modes, z_stiffness):
    bx, by, nz = vel_x.shape
    gx, gy = lax.axis_size("gx"), lax.axis_size("gy")
    peers = gx * gy
    each = nz // peers
    lanes = 2 * (bx + by)
    total_x, total_y = gx * bx, gy * by

    own_pack, narrow_pack, full_pack = Pack(np.float32), Pack(BF16), Pack(np.float32)
    own_pack.add("eig_x", np.broadcast_to(wall_eigen(bx)[:, None], (bx, nz)))
    own_pack.add("eig_y", np.broadcast_to(wall_eigen(by)[:, None], (by, nz)))
    for name, table in zip(FACTORS, local_tables(bx, by)):
        own_pack.add(name, table)

    near_x, cos_x, sin_x = phase_tables(gy, by)
    near_y, cos_y, sin_y = phase_tables(gx, bx)
    row_x, row_y = np.arange(peers) // gy, np.arange(peers) % gy
    full_pack.add("eig", eigen(total_x)[:, None] + eigen(total_y)[None, :])
    full_pack.add("far_xc", cos_x[row_y])
    full_pack.add("far_xs", sin_x[row_y])
    full_pack.add("far_yc", np.tile(cos_y[row_x], (each, 1)).T)
    full_pack.add("far_ys", np.tile(sin_y[row_x], (each, 1)).T)
    ahead_x, behind_x = edge_rows(gx, bx)
    ahead_y, behind_y = edge_rows(gy, by)
    ux = np.concatenate([ahead_x[row_x], behind_x[row_x]], 0)
    uy = np.concatenate([ahead_y[row_y], behind_y[row_y]], 0)
    uyt = np.concatenate([np.tile(table[row_y], (each, 1)).T for table in (ahead_y, behind_y)], 1)
    nxt = np.zeros((2, 2 * total_y, lanes))
    for face in range(2):
        nxt[face, :, face * by : (face + 1) * by] = near_x.T
    nxt = nxt.reshape(4 * total_y, lanes)
    stack_pair(narrow_pack, "nx", near_x)
    high, low = halves(near_y.T)
    narrow_pack.add("ny_stack", np.concatenate([high, high, low], 1))
    for name, table in (("nxt", nxt), ("nyt", near_y), ("uy", uy), ("ux", ux), ("uyt", uyt)):
        stack_pair(narrow_pack, name, table)
    narrow_pack.add("uxt", np.concatenate(list(halves(ux.T)), 1))

    args = [
        density, vel_x, vel_y, vel_z, own_pack.array(), z_stiffness.reshape(1, nz), z_modes,
        narrow_pack.array(), full_pack.array(),
    ]
    parts = LOADS
    cells = ((bx, by, nz), F32)
    traces = ((peers, each, lanes), F32)
    tables = [
        ((2, GROUP * by, GROUP * by), BF16), ((2, GROUP * bx, GROUP * bx), BF16),
        ((2, by // GROUP, GROUP * bx, lanes), BF16),
    ]
    hat, sent, scale, own, along_y, along_x, back, *kept = call(
        functools.partial(first_kernel, gx, gy, own_pack, parts, len(args)),
        [cells, traces, cells, ((each, total_y), F32), *tables] + [(arg.shape, arg.dtype) for arg in args],
        [
            pltpu.VMEM((bx, by, nz), F32),
            pltpu.VMEM((bx + by, nz), F32),
            pltpu.VMEM((2, by // GROUP, lanes, GROUP * bx), BF16),
            pltpu.SemaphoreType.DMA((parts, 4)),
            pltpu.SemaphoreType.DMA((len(args) - 4,)),
        ],
        args,
        in_space=pltpu.HBM,
    )
    got = lax.all_to_all(sent, ("gx", "gy"), 0, 0, tiled=True)
    rho, vx, vy, vz = kept[:4]
    zm, narrow, full = kept[6:]
    (solved,) = call(
        functools.partial(middle_kernel, gx, gy, bx, by, narrow_pack, full_pack),
        [traces],
        [],
        (got, own, narrow, full),
    )
    flux = lax.all_to_all(solved, ("gx", "gy"), 0, 0, tiled=True)
    block = pltpu.VMEM((bx, by, nz), F32)
    return call(
        functools.partial(last_kernel, gx, gy),
        [cells] * 3,
        [block] * 4 + [pltpu.SemaphoreType.DMA((bx // GROUP, 3))],
        (flux, hat, scale, rho, vx, vy, vz, zm, along_y, along_x, back),
        out_space=pltpu.HBM,
    )


def from_behind(block, axis, distance):
    devices = range(lax.axis_size(axis))
    route = [(i - distance, i) for i in devices if i - distance in devices]
    return lax.ppermute(block, axis, route)


def cosine_table(length):
    rows = lax.broadcasted_iota(jnp.int32, (length, length), 0)
    cols = lax.broadcasted_iota(jnp.int32, (length, length), 1)
    phase = rows * (2 * cols + 1) % (4 * length)
    angle = phase.astype(jnp.float32) * (math.pi / (2 * length))
    scales = jnp.where(rows == 0, math.sqrt(1.0 / length), math.sqrt(2.0 / length))
    return scales * jnp.cos(angle)


def upper_step(values):
    padding = [(0, 0)] * (values.ndim - 1) + [(0, 1)]
    return jnp.pad(values[..., 1:], padding) - values


def lower_step(values):
    padding = [(0, 0)] * (values.ndim - 1) + [(1, 0)]
    return values - jnp.pad(values[..., :-1], padding)


def eigenvalues(modes, length):
    return -(2.0 - 2.0 * jnp.cos(jnp.pi * modes / length))


def by_transposes(density, vel_x, vel_y, vel_z, z_modes, z_stiffness):
    cells_x = vel_x.shape[0]
    cells_y = vel_x.shape[1]
    depth = vel_x.shape[2]
    groups_x = lax.axis_size("gx")
    groups_y = lax.axis_size("gy")
    total_x = cells_x * groups_x
    total_y = cells_y * groups_y
    planes_dev = depth // groups_x
    xmodes_dev = total_x // groups_y
    table_x = cosine_table(total_x)
    table_y = cosine_table(total_y)
    heaviness = density.astype(jnp.float32)
    momentum_x = heaviness * vel_x
    momentum_y = heaviness * vel_y
    momentum_z = heaviness * vel_z
    below_x = from_behind(momentum_x[cells_x - 1 :], "gx", 1)
    below_y = from_behind(momentum_y[:, cells_y - 1 :], "gy", 1)
    diff_x = momentum_x - jnp.concatenate([below_x, momentum_x[:-1]], 0)
    diff_y = momentum_y - jnp.concatenate([below_y, momentum_y[:, :-1]], 1)
    source = diff_x + diff_y + lower_step(momentum_z)
    vertical = jnp.dot(source.reshape(cells_x * cells_y, depth), z_modes, precision=HIGHEST)
    vertical = vertical.reshape(cells_x, cells_y, groups_x, planes_dev).transpose(0, 2, 1, 3)
    vertical = vertical.reshape(cells_x, groups_x, cells_y * planes_dev)
    lines_x = lax.all_to_all(vertical, "gx", split_axis=1, concat_axis=0, tiled=True)
    lines_x = lines_x.reshape(total_x, cells_y, planes_dev)
    mixed = jnp.einsum("xyk,ax->yak", lines_x, table_x, precision=HIGHEST)
    mixed = mixed.reshape(cells_y, groups_y, xmodes_dev * planes_dev)
    lines_y = lax.all_to_all(mixed, "gy", split_axis=1, concat_axis=0, tiled=True)
    right_side = lines_y.reshape(total_y, xmodes_dev * planes_dev)
    spectrum = jnp.dot(table_y, right_side, precision=HIGHEST)
    z_first = lax.axis_index("gx") * planes_dev
    stiff_dev = lax.dynamic_slice_in_dim(z_stiffness, z_first, planes_dev)
    x_first = lax.axis_index("gy") * xmodes_dev
    modes_x = (x_first + jnp.arange(xmodes_dev, dtype=jnp.int32)).astype(jnp.float32)
    modes_y = jnp.arange(total_y, dtype=jnp.int32).astype(jnp.float32)
    divisor = (
        eigenvalues(modes_x, total_x)[None, :, None]
        + eigenvalues(modes_y, total_y)[:, None, None]
        - stiff_dev[None, None, :]
    )
    pressure_hat = spectrum / divisor.reshape(total_y, xmodes_dev * planes_dev)
    y_space = jnp.einsum("by,bc->yc", table_y, pressure_hat, precision=HIGHEST)
    modes_split = z_modes.reshape(depth, groups_x, planes_dev)
    sent_y = y_space.reshape(total_y, 1, xmodes_dev * planes_dev)
    lines_back = lax.all_to_all(sent_y, "gy", split_axis=0, concat_axis=1, tiled=True)
    lines_back = lines_back.reshape(cells_y, total_x, planes_dev)
    space_x = jnp.einsum("yak,ax->xyk", lines_back, table_x, precision=HIGHEST)
    sent_x = space_x.reshape(total_x, 1, cells_y * planes_dev)
    blocks = lax.all_to_all(sent_x, "gx", split_axis=0, concat_axis=1, tiled=True)
    blocks = blocks.reshape(cells_x, groups_x, cells_y, planes_dev)
    pressure = jnp.einsum("xhyk,zhk->xyz", blocks, modes_split, precision=HIGHEST)
    rim_x = from_behind(pressure[0:1], "gx", -1)
    grad_x = jnp.concatenate([pressure[1:], rim_x], 0) - pressure
    rim_y = from_behind(pressure[:, 0:1], "gy", -1)
    grad_y = jnp.concatenate([pressure[:, 1:], rim_y], 1) - pressure
    grad_z = upper_step(pressure)
    new_x = vel_x - grad_x / heaviness
    new_y = vel_y - grad_y / heaviness
    new_z = vel_z - grad_z / heaviness
    return (new_x, new_y, new_z)


def solution(mesh):
    sizes = mesh.shape
    peers = sizes["gx"] * sizes["gy"]

    def local(density, vel_x, vel_y, vel_z, z_modes, z_stiffness):
        cells_x, cells_y, depth = vel_x.shape
        total_x, total_y = cells_x * sizes["gx"], cells_y * sizes["gy"]
        fits = depth % peers == 0 and depth % 128 == 0 and 4 * peers % 128 == 0
        fits = fits and cells_x % (2 * GROUP) == 0 and cells_y % (2 * GROUP) == 0
        fits = fits and total_x % 128 == 0 and total_y % 128 == 0 and 3 * cells_x <= 128
        fits = fits and 2 * (cells_x + cells_y) % 128 == 0
        plan = by_faces if fits else by_transposes
        return tuple(plan(density, vel_x, vel_y, vel_z, z_modes, z_stiffness))

    block = P("gx", "gy", None)
    return jax.shard_map(
        local,
        mesh=mesh,
        in_specs=(block, block, block, block, P(), P()),
        out_specs=(block, block, block),
        check_vma=False,
    )
```

```python
import functools
import math

import jax
import jax.numpy as jnp
import numpy as np
from jax import lax
from jax.experimental import pallas as pl
from jax.experimental.pallas import tpu as pltpu
from jax.sharding import PartitionSpec as P

HIGHEST = lax.Precision.HIGHEST
F32 = jnp.float32
BF16 = jnp.bfloat16
GROUP = 8
GRANT = 16 << 20
LOADS = 1
FACTORS = ("rows_x", "rows_y", "faces_x", "faces_y")


def cosine(length):
    rows = np.arange(length)[:, None]
    cols = np.arange(length)[None, :]
    table = np.sqrt(2.0 / length) * np.cos(np.pi * rows * (2 * cols + 1) / (2 * length))
    table[0] = math.sqrt(1.0 / length)
    return table


def eigen(length):
    return -4.0 * np.sin(np.pi * np.arange(length) / (2 * length)) ** 2


def halves(table):
    table = np.asarray(table, np.float64)
    high = table.astype(np.float32).astype(BF16)
    low = (table - high.astype(np.float64)).astype(np.float32).astype(BF16)
    return np.stack([high, low])


def sine(length):
    modes = np.arange(1, length + 1)
    return np.sqrt(2.0 / (length + 1)) * np.sin(np.pi * np.outer(modes, modes) / (length + 1))


def wall_eigen(length):
    return -4.0 * np.sin(np.pi * np.arange(1, length + 1) / (2 * (length + 1))) ** 2


def local_tables(bx, by):
    sx, sy = sine(bx), sine(by)
    rows_x = np.repeat(sx, GROUP, 1)
    rows_y = np.tile(sy, (1, GROUP))
    faces_x = np.concatenate(
        [np.tile(sx[:, -1:], (1, by)), np.tile(sx[:, :1], (1, by)), sx, sx], 1
    )
    faces_y = np.concatenate(
        [sy, sy, np.tile(sy[:, -1:], (1, bx)), np.tile(sy[:, :1], (1, bx))], 1
    )
    return rows_x, rows_y, faces_x, faces_y


def edge_rows(blocks, size):
    table = cosine(blocks * size)
    ahead = np.minimum(size * (np.arange(blocks) + 1), blocks * size - 1)
    behind = np.maximum(size * np.arange(blocks) - 1, 0)
    return table[:, ahead].T, table[:, behind].T


def phase_tables(blocks, size):
    total = blocks * size
    modes = np.arange(total)
    scale = np.where(modes == 0, math.sqrt(1.0 / total), math.sqrt(2.0 / total))
    near = np.pi * np.outer(2 * np.arange(size) + 1, modes) / (2 * total)
    far = np.pi * np.outer(np.arange(blocks), modes) * size / total
    near = np.concatenate([scale * np.cos(near), scale * np.sin(near)], 1)
    return near, np.cos(far), np.sin(far)


class Pack:
    def __init__(self, kind):
        self.kind, self.rows, self.parts, self.places = kind, 0, [], {}

    def add(self, name, table):
        height, width = table.shape
        wide = -(-width // 128) * 128
        table = np.pad(np.asarray(table), ((0, 0), (0, wide - width)))
        self.places[name] = (self.rows, height, wide // 128)
        for first in range(0, wide, 128):
            self.parts.append(table[:, first : first + 128].astype(self.kind))
            self.rows += height
        assert height % 16 == 0

    def array(self):
        return jnp.asarray(np.concatenate(self.parts, 0))

    def read(self, ref, name):
        first, height, count = self.places[name]
        parts = [ref[first + i * height : first + (i + 1) * height, :] for i in range(count)]
        return parts[0] if count == 1 else jnp.concatenate(parts, 1)


def stack_pair(pack, name, table):
    high, low = halves(table)
    pack.add(name + "_high", high)
    pack.add(name + "_low", low)


def split(values):
    high = values.astype(BF16)
    low = (values - high.astype(F32)).astype(BF16)
    return high, low


def dot(left, right):
    return lax.dot_general(left, right, (((1,), (0,)), ((), ())), preferred_element_type=F32)


def mm(left, right):
    return dot(
        jnp.concatenate([left[0], left[1], left[0]], 1),
        jnp.concatenate([right[0], right[0], right[1]], 0),
    )


def widen(right):
    high, low = right
    return jnp.concatenate(
        [side_by_side([high, low]), side_by_side([high, jnp.zeros_like(low)])], 0
    )


def narrow_mm(left, wide):
    both = dot(side_by_side([left[0], left[1]]), wide)
    half = both.shape[1] // 2
    return both[:, :half] + both[:, half:]


def pair(ref, *index):
    return ref[(0, *index)], ref[(1, *index)]


def side_by_side(blocks):
    return jnp.concatenate(blocks, 1)


def iota(shape, dim):
    return lax.broadcasted_iota(jnp.int32, shape, dim)


def build_tables(rows_x, rows_y, faces_x, faces_y, ay_ref, ax_ref, back_ref, face_ref):
    bx, by = rows_x.shape[0], rows_y.shape[0]

    def halves_of(values):
        high = values.astype(BF16).astype(F32)
        return high, values - high

    for which, values in enumerate(halves_of(rows_y)):
        lane = iota(values.shape, 1)
        for k in range(GROUP):
            rows = slice(k * by, (k + 1) * by)
            ay_ref[which, rows, :] = jnp.where(lane // by == k, values, 0.0).astype(BF16)
    for which, values in enumerate(halves_of(rows_x)):
        shape = (GROUP, values.shape[1])
        same = iota(shape, 1) % GROUP == iota(shape, 0)
        for a in range(0, bx, 2):
            rows = [
                jnp.where(same, jnp.broadcast_to(values[i : i + 1, :], shape), 0.0)
                for i in (a, a + 1)
            ]
            rows = jnp.concatenate(rows, 0).astype(BF16)
            ax_ref[which, a * GROUP : (a + 2) * GROUP, :] = rows
    for group in range(by // GROUP):
        along = faces_y[group * GROUP : (group + 1) * GROUP, :]
        rows = jnp.concatenate([along * faces_x[a : a + 1, :] for a in range(bx)], 0)
        for which, part in enumerate(split(-rows)):
            back_ref[which, group] = part
        for which, part in enumerate(split(rows.T)):
            face_ref[which, group] = part


def first_kernel(
    gx, gy, pack, parts, count, *refs,
):
    hbm, refs = refs[:count], refs[count:]
    hat_ref, out_ref, scale_ref, own_ref, ay_ref, ax_ref, back_ref = refs[:7]
    kept, refs = refs[7 : 7 + count], refs[7 + count :]
    stage, edge, face_ref, cell_sems, table_sems = refs
    rho_ref, vx_ref, vy_ref, vz_ref, own_tables, zs_ref, zm_ref = kept[:7]
    bx, by, nz = vx_ref.shape
    step = 2 * GROUP
    size = bx // parts
    loads = []
    for part in range(parts):
        rows = pl.ds(part * size, size)
        loads.append(
            [
                pltpu.make_async_copy(hbm[i].at[rows], kept[i].at[rows], cell_sems.at[part, i])
                for i in range(4)
            ]
        )
    tables = {
        i: pltpu.make_async_copy(hbm[i], kept[i], table_sems.at[i - 4]) for i in range(4, count)
    }
    order = [tables[4], tables[5], *loads[0], tables[6]]
    for more in loads[1:]:
        order += more
    for load in order:
        load.start()

    cut_x = (lax.axis_index("gx") < gx - 1).astype(F32)
    cut_y = (lax.axis_index("gy") < gy - 1).astype(F32)
    row = iota((by, nz), 0)
    lane = iota((by, nz), 1)

    tables[4].wait()
    tables[5].wait()
    me = lax.axis_index("gx") * gy + lax.axis_index("gy")
    each = out_ref.shape[1]
    for c in range(each):
        mine = jnp.where(iota((1, nz), 1) == me * each + c, zs_ref[...], 0.0)
        mine = jnp.sum(mine, 1, keepdims=True)
        own_ref[c : c + 1, :] = jnp.broadcast_to(mine, (1, own_ref.shape[1]))
    eig_x, eig_y = pack.read(own_tables, "eig_x"), pack.read(own_tables, "eig_y")
    for a in range(bx):
        scale_ref[a] = 1.0 / (eig_y - zs_ref[...] + eig_x[a : a + 1, :])
    factors = [pack.read(own_tables, name) for name in FACTORS]
    build_tables(*factors, ay_ref, ax_ref, back_ref, face_ref)

    def source(start, previous):
        layers = []
        for x in range(start, start + GROUP):
            rho = rho_ref[x].astype(F32)
            mx = rho * vx_ref[x]
            my = rho * vy_ref[x]
            mz = rho * vz_ref[x]
            total = mx if previous is None else mx - previous
            previous = mx
            below = jnp.where(row == 0, 0.0, pltpu.roll(my, 1, 0))
            total = total + (my - below)
            under = jnp.where(lane == 0, 0.0, pltpu.roll(mz, 1, 1))
            total = total + (mz - under)
            layers.append(total)
            edge[by + x : by + x + 1, :] = my[by - 1 :, :] * cut_y
            if x == bx - 1:
                edge[0:by, :] = mx * cut_x
        return split(jnp.concatenate(layers, 0)), previous

    previous = None
    zm = None
    lines = []
    for start in range(0, bx, step):
        if start % size == 0:
            for load in loads[start // size]:
                load.wait()
            if start // size == parts - 1:
                for i in range(7, count):
                    tables[i].start()
            if zm is None:
                tables[6].wait()
                zm = widen(split(zm_ref[...]))
        lines = []
        for first in (start, start + GROUP):
            values, previous = source(first, previous)
            lines.append(narrow_mm(values, zm))
        block = mm((ay_ref[0], ay_ref[1]), split(side_by_side(lines)))
        stage[start : start + GROUP] = block[:, :nz].reshape(GROUP, by, nz)
        stage[start + GROUP : start + step] = block[:, nz:].reshape(GROUP, by, nz)
    momentum = narrow_mm(split(edge[...]), zm)
    mxs, mys = momentum[:by], momentum[by:]
    traces = jnp.concatenate([mxs, jnp.zeros_like(mxs), mys, jnp.zeros_like(mys)], 0)
    for start in range(0, by, step):
        groups = [slice(start, start + GROUP), slice(start + GROUP, start + step)]
        block = side_by_side([stage[:, rows, :].reshape(bx * GROUP, nz) for rows in groups])
        block = mm(pair(ax_ref), split(block))
        for which, rows in enumerate(groups):
            part = block[:, which * nz : (which + 1) * nz]
            hat_ref[:, rows, :] = part.reshape(bx, GROUP, nz)
            part = part * scale_ref[:, rows, :].reshape(bx * GROUP, nz)
            traces = traces + mm(pair(face_ref, rows.start // GROUP), split(part))
    turned = traces.T
    for peer in range(out_ref.shape[0]):
        out_ref[peer] = turned[peer * each : (peer + 1) * each, :]
    for i in range(7, count):
        tables[i].wait()


def middle_kernel(
    gx, gy, bx, by, narrow_pack, full_pack, in_ref, own_ref, narrow_ref, full_ref, out_ref,
):
    peers, each, lanes = in_ref.shape
    total_x, total_y = gx * bx, gy * by
    nz = peers * each
    blocks = [in_ref[:, c, :] for c in range(each)]
    data = jnp.concatenate(blocks, 0)
    turned = data.T

    def narrow(name):
        return narrow_pack.read(narrow_ref, name)

    def narrow_pair(name):
        return narrow(name + "_high"), narrow(name + "_low")

    def full(name):
        return full_pack.read(full_ref, name)

    near = []
    for part in narrow_pair("nx"):
        none = jnp.zeros_like(part)
        rest = jnp.zeros((2 * bx, 2 * part.shape[1]), BF16)
        near.append(
            jnp.concatenate([side_by_side([part, none]), side_by_side([none, part]), rest], 0)
        )
    wave = mm(split(data), near)
    far_xc, far_xs = full("far_xc"), full("far_xs")
    sides = []
    for face in range(2):
        base = 2 * total_y * face
        row_blocks = []
        for c in range(each):
            rows = slice(c * peers, (c + 1) * peers)
            cosine_part = wave[rows, base : base + total_y]
            sine_part = wave[rows, base + total_y : base + 2 * total_y]
            row_blocks.append(cosine_part * far_xc - sine_part * far_xs)
        sides.append(side_by_side(row_blocks))
    from_x = split(jnp.concatenate(sides, 0))

    first = 2 * by
    faces = side_by_side([turned[first : first + bx], turned[first + bx :]])
    high, low = split(faces)
    wave = dot(
        narrow("ny_stack"),
        jnp.concatenate([high, low, high, jnp.zeros((128 - 3 * bx, 2 * nz), BF16)], 0),
    )
    far_yc = side_by_side([full("far_yc")] * 2)
    far_ys = side_by_side([full("far_ys")] * 2)
    from_y = split(wave[:total_x] * far_yc - wave[total_x:] * far_ys)

    spread = []
    for part in narrow_pair("uy"):
        none = jnp.zeros((peers, total_y), BF16)
        rows = []
        for face in range(2):
            values = part[face * peers : (face + 1) * peers]
            for c in range(each):
                rows.append(side_by_side([values if c == k else none for k in range(each)]))
        spread.append(jnp.concatenate(rows, 0))
    uxt = narrow("uxt")
    spectrum = dot(
        side_by_side([from_y[0], from_y[1], from_y[0], uxt, uxt[:, : 2 * peers]]),
        jnp.concatenate(
            [spread[0], spread[0], spread[1], from_x[0], from_x[0], from_x[1]], 0
        ),
    )
    solved = []
    for c in range(each):
        divisor = full("eig") - own_ref[c : c + 1, :]
        solved.append(split(spectrum[:, c * total_y : (c + 1) * total_y] / divisor))
    high = side_by_side([part[0] for part in solved])
    low = side_by_side([part[1] for part in solved])

    along = mm(narrow_pair("ux"), (high, low))
    rows = []
    for c in range(each):
        columns = slice(c * total_y, (c + 1) * total_y)
        upper, lower = along[:peers, columns], along[peers:, columns]
        rows.append(side_by_side([upper * far_xc, -upper * far_xs, lower * far_xc, -lower * far_xs]))
    back = mm(split(jnp.concatenate(rows, 0)), narrow_pair("nxt"))

    lane = iota((total_x, 2 * nz), 1)
    owner = (lane % nz) // peers
    uyt = narrow_pair("uyt")
    along = None
    for c in range(each):
        part = mm(solved[c], uyt)
        along = part if along is None else jnp.where(owner == c, part, along)
    wave = split(jnp.concatenate([along * far_yc, -along * far_ys], 0))
    wave = mm(narrow_pair("nyt"), wave)
    other = jnp.concatenate([jnp.zeros((2 * by, nz), F32), wave[:, :nz], wave[:, nz:]], 0)
    back = back + other.T

    row = iota((peers, lanes), 0)
    lane = iota((peers, lanes), 1)
    row_x, row_y = row // gy, row % gy
    face = jnp.where(lane < by, 0, jnp.where(lane < 2 * by, 1, jnp.where(lane < 2 * by + bx, 2, 3)))
    coord = jnp.where(face < 2, row_x, row_y)
    end = jnp.where(face < 2, gx - 1, gy - 1)
    cut = jnp.where(face % 2 == 0, end - coord, coord) > 0
    for c in range(each):
        block = blocks[c]
        ahead, behind = pltpu.roll(block, lanes - by, 1), pltpu.roll(block, by, 1)
        ahead_x, behind_x = pltpu.roll(ahead, peers - gy, 0), pltpu.roll(behind, gy, 0)
        if bx != by:
            ahead, behind = pltpu.roll(block, lanes - bx, 1), pltpu.roll(block, bx, 1)
        ahead_y, behind_y = pltpu.roll(ahead, peers - 1, 0), pltpu.roll(behind, 1, 0)
        across = jnp.where(
            face == 0, ahead_x,
            jnp.where(face == 1, behind_x, jnp.where(face == 2, ahead_y, behind_y)),
        )
        across = jnp.where(cut, across, block)
        out_ref[:, c, :] = across - back[c * peers : (c + 1) * peers]


def last_kernel(
    gx, gy, flux_ref, hat_ref, scale_ref, rho_ref, vx_ref, vy_ref, vz_ref, zm_ref,
    ay_ref, ax_ref, back_ref, ox_hbm, oy_hbm, oz_hbm, ox_ref, oy_ref, oz_ref, stage, sems,
):
    bx, by, nz = vx_ref.shape
    step = 2 * GROUP
    last_x = lax.axis_index("gx") == gx - 1
    last_y = lax.axis_index("gy") == gy - 1
    zt = widen(split(zm_ref[...].T))
    flux = jnp.concatenate([flux_ref[peer] for peer in range(flux_ref.shape[0])], 0).T
    flux_parts = widen(split(flux))
    for start in range(0, by, step):
        blocks = []
        for rows in (slice(start, start + GROUP), slice(start + GROUP, start + step)):
            block = hat_ref[:, rows, :].reshape(bx * GROUP, nz)
            block = block + narrow_mm(pair(back_ref, rows.start // GROUP), flux_parts)
            blocks.append(block * scale_ref[:, rows, :].reshape(bx * GROUP, nz))
        block = mm(pair(ax_ref), split(side_by_side(blocks)))
        stage[:, start : start + GROUP, :] = block[:, :nz].reshape(bx, GROUP, nz)
        stage[:, start + GROUP : start + step, :] = block[:, nz:].reshape(bx, GROUP, nz)
    edges = narrow_mm(split(jnp.concatenate([flux[:by], flux[2 * by : 2 * by + bx]], 0)), zt)
    row = iota((by, nz), 0)
    lane = iota((by, nz), 1)
    layers = []
    stores = []
    done = 0
    for start in range(0, bx, step):
        parts = (slice(start, start + GROUP), slice(start + GROUP, start + step))
        block = side_by_side([stage[part].reshape(GROUP * by, nz) for part in parts])
        block = mm(pair(ay_ref), split(block))
        for which in range(2):
            values = narrow_mm(split(block[:, which * nz : (which + 1) * nz]), zt)
            layers += [values[i * by : (i + 1) * by] for i in range(GROUP)]
        ready = len(layers) if len(layers) == bx else len(layers) - GROUP
        for x in range(done, ready):
            here = layers[x]
            rho = 1.0 / rho_ref[x].astype(F32)
            if x < bx - 1:
                following = layers[x + 1]
            else:
                following = jnp.where(last_x, 0.0, edges[:by])
            ox_ref[x] = vx_ref[x] - (following - here) * rho
            cut = jnp.broadcast_to(edges[by + x : by + x + 1, :], (by, nz))
            cut = jnp.where(last_y, 0.0, cut)
            following = jnp.where(row == by - 1, cut, pltpu.roll(here, by - 1, 0))
            oy_ref[x] = vy_ref[x] - (following - here) * rho
            following = jnp.where(lane == nz - 1, 0.0, pltpu.roll(here, nz - 1, 1))
            oz_ref[x] = vz_ref[x] - (following - here) * rho
            if (x + 1) % GROUP == 0:
                part = x // GROUP
                rows = pl.ds(part * GROUP, GROUP)
                for i, (src, dst) in enumerate(
                    [(ox_ref, ox_hbm), (oy_ref, oy_hbm), (oz_ref, oz_hbm)]
                ):
                    store = pltpu.make_async_copy(src.at[rows], dst.at[rows], sems.at[part, i])
                    store.start()
                    stores.append(store)
        done = ready
    for store in stores:
        store.wait()


def call(kernel, outs, scratch, args, in_space=pltpu.VMEM, out_space=pltpu.VMEM):
    placed = [pltpu.with_memory_space_constraint(arg, in_space) for arg in args]
    return pl.pallas_call(
        kernel,
        out_shape=[out_space(shape, dtype) for shape, dtype in outs],
        in_specs=[pl.BlockSpec(memory_space=in_space)] * len(args),
        out_specs=[pl.BlockSpec(memory_space=out_space)] * len(outs),
        scratch_shapes=scratch,
        compiler_params=pltpu.CompilerParams(vmem_limit_bytes=GRANT),
    )(*placed)


def by_faces(density, vel_x, vel_y, vel_z, z_modes, z_stiffness):
    bx, by, nz = vel_x.shape
    gx, gy = lax.axis_size("gx"), lax.axis_size("gy")
    peers = gx * gy
    each = nz // peers
    lanes = 2 * (bx + by)
    total_x, total_y = gx * bx, gy * by

    own_pack, narrow_pack, full_pack = Pack(np.float32), Pack(BF16), Pack(np.float32)
    own_pack.add("eig_x", np.broadcast_to(wall_eigen(bx)[:, None], (bx, nz)))
    own_pack.add("eig_y", np.broadcast_to(wall_eigen(by)[:, None], (by, nz)))
    for name, table in zip(FACTORS, local_tables(bx, by)):
        own_pack.add(name, table)

    near_x, cos_x, sin_x = phase_tables(gy, by)
    near_y, cos_y, sin_y = phase_tables(gx, bx)
    row_x, row_y = np.arange(peers) // gy, np.arange(peers) % gy
    full_pack.add("eig", eigen(total_x)[:, None] + eigen(total_y)[None, :])
    full_pack.add("far_xc", cos_x[row_y])
    full_pack.add("far_xs", sin_x[row_y])
    full_pack.add("far_yc", np.tile(cos_y[row_x], (each, 1)).T)
    full_pack.add("far_ys", np.tile(sin_y[row_x], (each, 1)).T)
    ahead_x, behind_x = edge_rows(gx, bx)
    ahead_y, behind_y = edge_rows(gy, by)
    ux = np.concatenate([ahead_x[row_x], behind_x[row_x]], 0)
    uy = np.concatenate([ahead_y[row_y], behind_y[row_y]], 0)
    uyt = np.concatenate([np.tile(table[row_y], (each, 1)).T for table in (ahead_y, behind_y)], 1)
    nxt = np.zeros((2, 2 * total_y, lanes))
    for face in range(2):
        nxt[face, :, face * by : (face + 1) * by] = near_x.T
    nxt = nxt.reshape(4 * total_y, lanes)
    stack_pair(narrow_pack, "nx", near_x)
    high, low = halves(near_y.T)
    narrow_pack.add("ny_stack", np.concatenate([high, high, low], 1))
    for name, table in (("nxt", nxt), ("nyt", near_y), ("uy", uy), ("ux", ux), ("uyt", uyt)):
        stack_pair(narrow_pack, name, table)
    narrow_pack.add("uxt", np.concatenate(list(halves(ux.T)), 1))

    args = [
        density, vel_x, vel_y, vel_z, own_pack.array(), z_stiffness.reshape(1, nz), z_modes,
        narrow_pack.array(), full_pack.array(),
    ]
    parts = LOADS
    cells = ((bx, by, nz), F32)
    traces = ((peers, each, lanes), F32)
    tables = [
        ((2, GROUP * by, GROUP * by), BF16), ((2, GROUP * bx, GROUP * bx), BF16),
        ((2, by // GROUP, GROUP * bx, lanes), BF16),
    ]
    hat, sent, scale, own, along_y, along_x, back, *kept = call(
        functools.partial(first_kernel, gx, gy, own_pack, parts, len(args)),
        [cells, traces, cells, ((each, total_y), F32), *tables] + [(arg.shape, arg.dtype) for arg in args],
        [
            pltpu.VMEM((bx, by, nz), F32),
            pltpu.VMEM((bx + by, nz), F32),
            pltpu.VMEM((2, by // GROUP, lanes, GROUP * bx), BF16),
            pltpu.SemaphoreType.DMA((parts, 4)),
            pltpu.SemaphoreType.DMA((len(args) - 4,)),
        ],
        args,
        in_space=pltpu.HBM,
    )
    got = lax.all_to_all(sent, ("gx", "gy"), 0, 0, tiled=True)
    rho, vx, vy, vz = kept[:4]
    zm, narrow, full = kept[6:]
    (solved,) = call(
        functools.partial(middle_kernel, gx, gy, bx, by, narrow_pack, full_pack),
        [traces],
        [],
        (got, own, narrow, full),
    )
    flux = lax.all_to_all(solved, ("gx", "gy"), 0, 0, tiled=True)
    block = pltpu.VMEM((bx, by, nz), F32)
    return call(
        functools.partial(last_kernel, gx, gy),
        [cells] * 3,
        [block] * 4 + [pltpu.SemaphoreType.DMA((bx // GROUP, 3))],
        (flux, hat, scale, rho, vx, vy, vz, zm, along_y, along_x, back),
        out_space=pltpu.HBM,
    )


def from_behind(block, axis, distance):
    devices = range(lax.axis_size(axis))
    route = [(i - distance, i) for i in devices if i - distance in devices]
    return lax.ppermute(block, axis, route)


def cosine_table(length):
    rows = lax.broadcasted_iota(jnp.int32, (length, length), 0)
    cols = lax.broadcasted_iota(jnp.int32, (length, length), 1)
    phase = rows * (2 * cols + 1) % (4 * length)
    angle = phase.astype(jnp.float32) * (math.pi / (2 * length))
    scales = jnp.where(rows == 0, math.sqrt(1.0 / length), math.sqrt(2.0 / length))
    return scales * jnp.cos(angle)


def upper_step(values):
    padding = [(0, 0)] * (values.ndim - 1) + [(0, 1)]
    return jnp.pad(values[..., 1:], padding) - values


def lower_step(values):
    padding = [(0, 0)] * (values.ndim - 1) + [(1, 0)]
    return values - jnp.pad(values[..., :-1], padding)


def eigenvalues(modes, length):
    return -(2.0 - 2.0 * jnp.cos(jnp.pi * modes / length))


def by_transposes(density, vel_x, vel_y, vel_z, z_modes, z_stiffness):
    cells_x = vel_x.shape[0]
    cells_y = vel_x.shape[1]
    depth = vel_x.shape[2]
    groups_x = lax.axis_size("gx")
    groups_y = lax.axis_size("gy")
    total_x = cells_x * groups_x
    total_y = cells_y * groups_y
    planes_dev = depth // groups_x
    xmodes_dev = total_x // groups_y
    table_x = cosine_table(total_x)
    table_y = cosine_table(total_y)
    heaviness = density.astype(jnp.float32)
    momentum_x = heaviness * vel_x
    momentum_y = heaviness * vel_y
    momentum_z = heaviness * vel_z
    below_x = from_behind(momentum_x[cells_x - 1 :], "gx", 1)
    below_y = from_behind(momentum_y[:, cells_y - 1 :], "gy", 1)
    diff_x = momentum_x - jnp.concatenate([below_x, momentum_x[:-1]], 0)
    diff_y = momentum_y - jnp.concatenate([below_y, momentum_y[:, :-1]], 1)
    source = diff_x + diff_y + lower_step(momentum_z)
    vertical = jnp.dot(source.reshape(cells_x * cells_y, depth), z_modes, precision=HIGHEST)
    vertical = vertical.reshape(cells_x, cells_y, groups_x, planes_dev).transpose(0, 2, 1, 3)
    vertical = vertical.reshape(cells_x, groups_x, cells_y * planes_dev)
    lines_x = lax.all_to_all(vertical, "gx", split_axis=1, concat_axis=0, tiled=True)
    lines_x = lines_x.reshape(total_x, cells_y, planes_dev)
    mixed = jnp.einsum("xyk,ax->yak", lines_x, table_x, precision=HIGHEST)
    mixed = mixed.reshape(cells_y, groups_y, xmodes_dev * planes_dev)
    lines_y = lax.all_to_all(mixed, "gy", split_axis=1, concat_axis=0, tiled=True)
    right_side = lines_y.reshape(total_y, xmodes_dev * planes_dev)
    spectrum = jnp.dot(table_y, right_side, precision=HIGHEST)
    z_first = lax.axis_index("gx") * planes_dev
    stiff_dev = lax.dynamic_slice_in_dim(z_stiffness, z_first, planes_dev)
    x_first = lax.axis_index("gy") * xmodes_dev
    modes_x = (x_first + jnp.arange(xmodes_dev, dtype=jnp.int32)).astype(jnp.float32)
    modes_y = jnp.arange(total_y, dtype=jnp.int32).astype(jnp.float32)
    divisor = (
        eigenvalues(modes_x, total_x)[None, :, None]
        + eigenvalues(modes_y, total_y)[:, None, None]
        - stiff_dev[None, None, :]
    )
    pressure_hat = spectrum / divisor.reshape(total_y, xmodes_dev * planes_dev)
    y_space = jnp.einsum("by,bc->yc", table_y, pressure_hat, precision=HIGHEST)
    modes_split = z_modes.reshape(depth, groups_x, planes_dev)
    sent_y = y_space.reshape(total_y, 1, xmodes_dev * planes_dev)
    lines_back = lax.all_to_all(sent_y, "gy", split_axis=0, concat_axis=1, tiled=True)
    lines_back = lines_back.reshape(cells_y, total_x, planes_dev)
    space_x = jnp.einsum("yak,ax->xyk", lines_back, table_x, precision=HIGHEST)
    sent_x = space_x.reshape(total_x, 1, cells_y * planes_dev)
    blocks = lax.all_to_all(sent_x, "gx", split_axis=0, concat_axis=1, tiled=True)
    blocks = blocks.reshape(cells_x, groups_x, cells_y, planes_dev)
    pressure = jnp.einsum("xhyk,zhk->xyz", blocks, modes_split, precision=HIGHEST)
    rim_x = from_behind(pressure[0:1], "gx", -1)
    grad_x = jnp.concatenate([pressure[1:], rim_x], 0) - pressure
    rim_y = from_behind(pressure[:, 0:1], "gy", -1)
    grad_y = jnp.concatenate([pressure[:, 1:], rim_y], 1) - pressure
    grad_z = upper_step(pressure)
    new_x = vel_x - grad_x / heaviness
    new_y = vel_y - grad_y / heaviness
    new_z = vel_z - grad_z / heaviness
    return (new_x, new_y, new_z)


def solution(mesh):
    sizes = mesh.shape
    peers = sizes["gx"] * sizes["gy"]

    def local(density, vel_x, vel_y, vel_z, z_modes, z_stiffness):
        cells_x, cells_y, depth = vel_x.shape
        total_x, total_y = cells_x * sizes["gx"], cells_y * sizes["gy"]
        fits = depth % peers == 0 and depth % 128 == 0 and 4 * peers % 128 == 0
        fits = fits and cells_x % (2 * GROUP) == 0 and cells_y % (2 * GROUP) == 0
        fits = fits and total_x % 128 == 0 and total_y % 128 == 0 and 3 * cells_x <= 128
        fits = fits and 2 * (cells_x + cells_y) % 128 == 0
        plan = by_faces if fits else by_transposes
        return tuple(plan(density, vel_x, vel_y, vel_z, z_modes, z_stiffness))

    block = P("gx", "gy", None)
    return jax.shard_map(
        local,
        mesh=mesh,
        in_specs=(block, block, block, block, P(), P()),
        out_specs=(block, block, block),
        check_vma=False,
    )
```

```python
import functools
import math

import jax
import jax.numpy as jnp
import numpy as np
from jax import lax
from jax.experimental import pallas as pl
from jax.experimental.pallas import tpu as pltpu
from jax.sharding import PartitionSpec as P

HIGHEST = lax.Precision.HIGHEST
F32 = jnp.float32
BF16 = jnp.bfloat16
GROUP = 8
GRANT = 16 << 20
LOADS = 1
FACTORS = ("rows_x", "rows_y", "faces_x", "faces_y")


def cosine(length):
    rows = np.arange(length)[:, None]
    cols = np.arange(length)[None, :]
    table = np.sqrt(2.0 / length) * np.cos(np.pi * rows * (2 * cols + 1) / (2 * length))
    table[0] = math.sqrt(1.0 / length)
    return table


def eigen(length):
    return -4.0 * np.sin(np.pi * np.arange(length) / (2 * length)) ** 2


def sine(length):
    modes = np.arange(1, length + 1)
    return np.sqrt(2.0 / (length + 1)) * np.sin(np.pi * np.outer(modes, modes) / (length + 1))


def wall_eigen(length):
    return -4.0 * np.sin(np.pi * np.arange(1, length + 1) / (2 * (length + 1))) ** 2


def local_tables(bx, by):
    sx, sy = sine(bx), sine(by)
    rows_x = np.repeat(sx, GROUP, 1)
    rows_y = np.tile(sy, (1, GROUP))
    faces_x = np.concatenate(
        [np.tile(sx[:, -1:], (1, by)), np.tile(sx[:, :1], (1, by)), sx, sx], 1
    )
    faces_y = np.concatenate(
        [sy, sy, np.tile(sy[:, -1:], (1, bx)), np.tile(sy[:, :1], (1, bx))], 1
    )
    return rows_x, rows_y, faces_x, faces_y


def edge_rows(blocks, size):
    table = cosine(blocks * size)
    ahead = np.minimum(size * (np.arange(blocks) + 1), blocks * size - 1)
    behind = np.maximum(size * np.arange(blocks) - 1, 0)
    return table[:, ahead].T, table[:, behind].T


def phase_tables(blocks, size):
    total = blocks * size
    modes = np.arange(total)
    scale = np.where(modes == 0, math.sqrt(1.0 / total), math.sqrt(2.0 / total))
    near = np.pi * np.outer(2 * np.arange(size) + 1, modes) / (2 * total)
    far = np.pi * np.outer(np.arange(blocks), modes) * size / total
    near = np.concatenate([scale * np.cos(near), scale * np.sin(near)], 1)
    return near, np.cos(far), np.sin(far)


class Pack:
    def __init__(self, kind):
        self.kind, self.rows, self.parts, self.places = kind, 0, [], {}

    def add(self, name, table):
        height, width = table.shape
        wide = -(-width // 128) * 128
        table = np.pad(np.asarray(table), ((0, 0), (0, wide - width)))
        self.places[name] = (self.rows, height, wide // 128)
        for first in range(0, wide, 128):
            self.parts.append(table[:, first : first + 128].astype(self.kind))
            self.rows += height
        assert height % 16 == 0

    def array(self):
        return jnp.asarray(np.concatenate(self.parts, 0))

    def read(self, ref, name):
        first, height, count = self.places[name]
        parts = [ref[first + i * height : first + (i + 1) * height, :] for i in range(count)]
        return parts[0] if count == 1 else jnp.concatenate(parts, 1)


def split(values):
    high = values.astype(BF16)
    low = (values - high.astype(F32)).astype(BF16)
    return high, low


def dot(left, right):
    return lax.dot_general(left, right, (((1,), (0,)), ((), ())), preferred_element_type=F32)


def mm(left, right):
    return dot(
        jnp.concatenate([left[0], left[1], left[0]], 1),
        jnp.concatenate([right[0], right[0], right[1]], 0),
    )


def widen(right):
    high, low = right
    return jnp.concatenate(
        [side_by_side([high, low]), side_by_side([high, jnp.zeros_like(low)])], 0
    )


def narrow_mm(left, wide):
    both = dot(side_by_side([left[0], left[1]]), wide)
    half = both.shape[1] // 2
    return both[:, :half] + both[:, half:]


def pair(ref, *index):
    return ref[(0, *index)], ref[(1, *index)]


def side_by_side(blocks):
    return jnp.concatenate(blocks, 1)


def iota(shape, dim):
    return lax.broadcasted_iota(jnp.int32, shape, dim)


def build_tables(rows_x, rows_y, faces_x, faces_y, ay_ref, ax_ref, back_ref, face_ref):
    bx, by = rows_x.shape[0], rows_y.shape[0]

    def halves_of(values):
        high = values.astype(BF16).astype(F32)
        return high, values - high

    for which, values in enumerate(halves_of(rows_y)):
        lane = iota(values.shape, 1)
        for k in range(GROUP):
            rows = slice(k * by, (k + 1) * by)
            ay_ref[which, rows, :] = jnp.where(lane // by == k, values, 0.0).astype(BF16)
    for which, values in enumerate(halves_of(rows_x)):
        shape = (GROUP, values.shape[1])
        same = iota(shape, 1) % GROUP == iota(shape, 0)
        for a in range(0, bx, 2):
            rows = [
                jnp.where(same, jnp.broadcast_to(values[i : i + 1, :], shape), 0.0)
                for i in (a, a + 1)
            ]
            rows = jnp.concatenate(rows, 0).astype(BF16)
            ax_ref[which, a * GROUP : (a + 2) * GROUP, :] = rows
    for group in range(by // GROUP):
        along = faces_y[group * GROUP : (group + 1) * GROUP, :]
        rows = jnp.concatenate([along * faces_x[a : a + 1, :] for a in range(bx)], 0)
        for which, part in enumerate(split(-rows)):
            back_ref[which, group] = part
        for which, part in enumerate(split(rows.T)):
            face_ref[which, group] = part


def build_middle(table, each, nx_ref, nxt_ref, ny_ref, nyt_ref, uy_ref, ux_ref, uxt_ref, uyt_ref, eig_ref, far_ref):
    near = table("near_x")
    size, width = near.shape
    lanes = nxt_ref.shape[2]
    nx_ref[0], nx_ref[1] = split(near)
    for face in range(2):
        rows = [near, jnp.zeros((lanes - (face + 1) * size, width), F32)]
        if face:
            rows = [jnp.zeros((face * size, width), F32)] + rows
        place = slice(face * width, (face + 1) * width)
        nxt_ref[0, place, :], nxt_ref[1, place, :] = split(jnp.concatenate(rows, 0).T)
    near = table("near_y")
    size, width = near.shape
    nyt_ref[0], nyt_ref[1] = split(near)
    high = near.astype(BF16).astype(F32)
    rows = [high, high, near - high, jnp.zeros((128 - 3 * size, width), F32)]
    ny_ref[...] = jnp.concatenate(rows, 0).T.astype(BF16)
    values = table("ux")
    ux_ref[0], ux_ref[1] = split(values)
    high = values.astype(BF16).astype(F32)
    uxt_ref[...] = jnp.concatenate([high, values - high], 0).T.astype(BF16)
    values = table("uy")
    uy_ref[0], uy_ref[1] = split(values)
    half = values.shape[0] // 2
    rows = jnp.concatenate([values[:half]] * each + [values[half:]] * each, 0)
    uyt_ref[0], uyt_ref[1] = split(rows.T)
    column = jnp.concatenate([table("line_x")] * 8, 0).T
    column = side_by_side([column] * (eig_ref.shape[1] // 128))
    eig_ref[...] = column + table("line_y")[:1]
    for which, name in enumerate(("far_yc", "far_ys")):
        far_ref[which] = jnp.concatenate([table(name)] * each, 0).T


def first_kernel(
    gx, gy, pack, parts, count, *refs,
):
    hbm, refs = refs[:count], refs[count:]
    hat_ref, out_ref, scale_ref, own_ref, ay_ref, ax_ref, back_ref = refs[:7]
    later, refs = refs[7:17], refs[17:]
    kept, refs = refs[:count], refs[count:]
    stage, edge, face_ref, cell_sems, table_sems = refs
    rho_ref, vx_ref, vy_ref, vz_ref, own_tables, zs_ref, zm_ref = kept[:7]
    bx, by, nz = vx_ref.shape
    step = 2 * GROUP
    size = bx // parts
    loads = []
    for part in range(parts):
        rows = pl.ds(part * size, size)
        loads.append(
            [
                pltpu.make_async_copy(hbm[i].at[rows], kept[i].at[rows], cell_sems.at[part, i])
                for i in range(4)
            ]
        )
    tables = {
        i: pltpu.make_async_copy(hbm[i], kept[i], table_sems.at[i - 4]) for i in range(4, count)
    }
    order = [tables[4], tables[5], *loads[0], tables[6]]
    for more in loads[1:]:
        order += more
    for load in order:
        load.start()

    cut_x = (lax.axis_index("gx") < gx - 1).astype(F32)
    cut_y = (lax.axis_index("gy") < gy - 1).astype(F32)
    row = iota((by, nz), 0)
    lane = iota((by, nz), 1)

    tables[4].wait()
    tables[5].wait()
    me = lax.axis_index("gx") * gy + lax.axis_index("gy")
    each = out_ref.shape[1]
    for c in range(each):
        mine = jnp.where(iota((1, nz), 1) == me * each + c, zs_ref[...], 0.0)
        mine = jnp.sum(mine, 1, keepdims=True)
        own_ref[c : c + 1, :] = jnp.broadcast_to(mine, (1, own_ref.shape[1]))
    eig_x, eig_y = pack.read(own_tables, "eig_x"), pack.read(own_tables, "eig_y")
    for a in range(bx):
        scale_ref[a] = 1.0 / (eig_y - zs_ref[...] + eig_x[a : a + 1, :])
    factors = [pack.read(own_tables, name) for name in FACTORS]
    build_tables(*factors, ay_ref, ax_ref, back_ref, face_ref)
    build_middle(functools.partial(pack.read, own_tables), each, *later)

    def source(start, previous):
        layers = []
        for x in range(start, start + GROUP):
            rho = rho_ref[x].astype(F32)
            mx = rho * vx_ref[x]
            my = rho * vy_ref[x]
            mz = rho * vz_ref[x]
            total = mx if previous is None else mx - previous
            previous = mx
            below = jnp.where(row == 0, 0.0, pltpu.roll(my, 1, 0))
            total = total + (my - below)
            under = jnp.where(lane == 0, 0.0, pltpu.roll(mz, 1, 1))
            total = total + (mz - under)
            layers.append(total)
            edge[by + x : by + x + 1, :] = my[by - 1 :, :] * cut_y
            if x == bx - 1:
                edge[0:by, :] = mx * cut_x
        return split(jnp.concatenate(layers, 0)), previous

    previous = None
    zm = None
    lines = []
    for start in range(0, bx, step):
        if start % size == 0:
            for load in loads[start // size]:
                load.wait()
            if zm is None:
                tables[6].wait()
                zm = widen(split(zm_ref[...]))
        lines = []
        for first in (start, start + GROUP):
            values, previous = source(first, previous)
            lines.append(narrow_mm(values, zm))
        block = mm((ay_ref[0], ay_ref[1]), split(side_by_side(lines)))
        stage[start : start + GROUP] = block[:, :nz].reshape(GROUP, by, nz)
        stage[start + GROUP : start + step] = block[:, nz:].reshape(GROUP, by, nz)
    momentum = narrow_mm(split(edge[...]), zm)
    mxs, mys = momentum[:by], momentum[by:]
    traces = jnp.concatenate([mxs, jnp.zeros_like(mxs), mys, jnp.zeros_like(mys)], 0)
    for start in range(0, by, step):
        groups = [slice(start, start + GROUP), slice(start + GROUP, start + step)]
        block = side_by_side([stage[:, rows, :].reshape(bx * GROUP, nz) for rows in groups])
        block = mm(pair(ax_ref), split(block))
        for which, rows in enumerate(groups):
            part = block[:, which * nz : (which + 1) * nz]
            hat_ref[:, rows, :] = part.reshape(bx, GROUP, nz)
            part = part * scale_ref[:, rows, :].reshape(bx * GROUP, nz)
            traces = traces + mm(pair(face_ref, rows.start // GROUP), split(part))
    turned = traces.T
    for peer in range(out_ref.shape[0]):
        out_ref[peer] = turned[peer * each : (peer + 1) * each, :]


def middle_kernel(
    gx, gy, bx, by, pack, in_ref, own_ref, own_tables,
    nx_ref, nxt_ref, ny_ref, nyt_ref, uy_ref, ux_ref, uxt_ref, uyt_ref, eig_ref, far_ref, out_ref,
):
    peers, each, lanes = in_ref.shape
    total_x, total_y = gx * bx, gy * by
    nz = peers * each
    blocks = [in_ref[:, c, :] for c in range(each)]
    data = jnp.concatenate(blocks, 0)
    turned = data.T

    near = []
    for part in pair(nx_ref):
        none = jnp.zeros_like(part)
        rest = jnp.zeros((2 * bx, 2 * part.shape[1]), BF16)
        near.append(
            jnp.concatenate([side_by_side([part, none]), side_by_side([none, part]), rest], 0)
        )
    wave = mm(split(data), near)
    far_xc, far_xs = pack.read(own_tables, "far_xc"), pack.read(own_tables, "far_xs")
    sides = []
    for face in range(2):
        base = 2 * total_y * face
        row_blocks = []
        for c in range(each):
            rows = slice(c * peers, (c + 1) * peers)
            cosine_part = wave[rows, base : base + total_y]
            sine_part = wave[rows, base + total_y : base + 2 * total_y]
            row_blocks.append(cosine_part * far_xc - sine_part * far_xs)
        sides.append(side_by_side(row_blocks))
    from_x = split(jnp.concatenate(sides, 0))

    first = 2 * by
    faces = side_by_side([turned[first : first + bx], turned[first + bx :]])
    high, low = split(faces)
    wave = dot(
        ny_ref[...],
        jnp.concatenate([high, low, high, jnp.zeros((128 - 3 * bx, 2 * nz), BF16)], 0),
    )
    far_yc = side_by_side([far_ref[0]] * 2)
    far_ys = side_by_side([far_ref[1]] * 2)
    from_y = split(wave[:total_x] * far_yc - wave[total_x:] * far_ys)

    spread = []
    for part in pair(uy_ref):
        none = jnp.zeros((peers, total_y), BF16)
        rows = []
        for face in range(2):
            values = part[face * peers : (face + 1) * peers]
            for c in range(each):
                rows.append(side_by_side([values if c == k else none for k in range(each)]))
        spread.append(jnp.concatenate(rows, 0))
    uxt = uxt_ref[...]
    spectrum = dot(
        side_by_side([from_y[0], from_y[1], from_y[0], uxt, uxt[:, : 2 * peers]]),
        jnp.concatenate(
            [spread[0], spread[0], spread[1], from_x[0], from_x[0], from_x[1]], 0
        ),
    )
    solved = []
    for c in range(each):
        divisor = eig_ref[...] - own_ref[c : c + 1, :]
        solved.append(split(spectrum[:, c * total_y : (c + 1) * total_y] / divisor))
    high = side_by_side([part[0] for part in solved])
    low = side_by_side([part[1] for part in solved])

    along = mm(pair(ux_ref), (high, low))
    rows = []
    for c in range(each):
        columns = slice(c * total_y, (c + 1) * total_y)
        upper, lower = along[:peers, columns], along[peers:, columns]
        rows.append(side_by_side([upper * far_xc, -upper * far_xs, lower * far_xc, -lower * far_xs]))
    back = mm(split(jnp.concatenate(rows, 0)), pair(nxt_ref))

    lane = iota((total_x, 2 * nz), 1)
    owner = (lane % nz) // peers
    uyt = pair(uyt_ref)
    along = None
    for c in range(each):
        part = mm(solved[c], uyt)
        along = part if along is None else jnp.where(owner == c, part, along)
    wave = split(jnp.concatenate([along * far_yc, -along * far_ys], 0))
    wave = mm(pair(nyt_ref), wave)
    other = jnp.concatenate([jnp.zeros((2 * by, nz), F32), wave[:, :nz], wave[:, nz:]], 0)
    back = back + other.T

    row = iota((peers, lanes), 0)
    lane = iota((peers, lanes), 1)
    row_x, row_y = row // gy, row % gy
    face = jnp.where(lane < by, 0, jnp.where(lane < 2 * by, 1, jnp.where(lane < 2 * by + bx, 2, 3)))
    coord = jnp.where(face < 2, row_x, row_y)
    end = jnp.where(face < 2, gx - 1, gy - 1)
    cut = jnp.where(face % 2 == 0, end - coord, coord) > 0
    for c in range(each):
        block = blocks[c]
        ahead, behind = pltpu.roll(block, lanes - by, 1), pltpu.roll(block, by, 1)
        ahead_x, behind_x = pltpu.roll(ahead, peers - gy, 0), pltpu.roll(behind, gy, 0)
        if bx != by:
            ahead, behind = pltpu.roll(block, lanes - bx, 1), pltpu.roll(block, bx, 1)
        ahead_y, behind_y = pltpu.roll(ahead, peers - 1, 0), pltpu.roll(behind, 1, 0)
        across = jnp.where(
            face == 0, ahead_x,
            jnp.where(face == 1, behind_x, jnp.where(face == 2, ahead_y, behind_y)),
        )
        across = jnp.where(cut, across, block)
        out_ref[:, c, :] = across - back[c * peers : (c + 1) * peers]


def last_kernel(
    gx, gy, flux_ref, hat_ref, scale_ref, rho_ref, vx_ref, vy_ref, vz_ref, zm_ref,
    ay_ref, ax_ref, back_ref, ox_hbm, oy_hbm, oz_hbm, ox_ref, oy_ref, oz_ref, stage, sems,
):
    bx, by, nz = vx_ref.shape
    step = 2 * GROUP
    last_x = lax.axis_index("gx") == gx - 1
    last_y = lax.axis_index("gy") == gy - 1
    zt = widen(split(zm_ref[...].T))
    flux = jnp.concatenate([flux_ref[peer] for peer in range(flux_ref.shape[0])], 0).T
    flux_parts = widen(split(flux))
    for start in range(0, by, step):
        blocks = []
        for rows in (slice(start, start + GROUP), slice(start + GROUP, start + step)):
            block = hat_ref[:, rows, :].reshape(bx * GROUP, nz)
            block = block + narrow_mm(pair(back_ref, rows.start // GROUP), flux_parts)
            blocks.append(block * scale_ref[:, rows, :].reshape(bx * GROUP, nz))
        block = mm(pair(ax_ref), split(side_by_side(blocks)))
        stage[:, start : start + GROUP, :] = block[:, :nz].reshape(bx, GROUP, nz)
        stage[:, start + GROUP : start + step, :] = block[:, nz:].reshape(bx, GROUP, nz)
    edges = narrow_mm(split(jnp.concatenate([flux[:by], flux[2 * by : 2 * by + bx]], 0)), zt)
    row = iota((by, nz), 0)
    lane = iota((by, nz), 1)
    layers = []
    stores = []
    done = 0
    for start in range(0, bx, step):
        parts = (slice(start, start + GROUP), slice(start + GROUP, start + step))
        block = side_by_side([stage[part].reshape(GROUP * by, nz) for part in parts])
        block = mm(pair(ay_ref), split(block))
        for which in range(2):
            values = narrow_mm(split(block[:, which * nz : (which + 1) * nz]), zt)
            layers += [values[i * by : (i + 1) * by] for i in range(GROUP)]
        ready = len(layers) if len(layers) == bx else len(layers) - GROUP
        for x in range(done, ready):
            here = layers[x]
            rho = 1.0 / rho_ref[x].astype(F32)
            if x < bx - 1:
                following = layers[x + 1]
            else:
                following = jnp.where(last_x, 0.0, edges[:by])
            ox_ref[x] = vx_ref[x] - (following - here) * rho
            cut = jnp.broadcast_to(edges[by + x : by + x + 1, :], (by, nz))
            cut = jnp.where(last_y, 0.0, cut)
            following = jnp.where(row == by - 1, cut, pltpu.roll(here, by - 1, 0))
            oy_ref[x] = vy_ref[x] - (following - here) * rho
            following = jnp.where(lane == nz - 1, 0.0, pltpu.roll(here, nz - 1, 1))
            oz_ref[x] = vz_ref[x] - (following - here) * rho
            if (x + 1) % GROUP == 0:
                part = x // GROUP
                rows = pl.ds(part * GROUP, GROUP)
                for i, (src, dst) in enumerate(
                    [(ox_ref, ox_hbm), (oy_ref, oy_hbm), (oz_ref, oz_hbm)]
                ):
                    store = pltpu.make_async_copy(src.at[rows], dst.at[rows], sems.at[part, i])
                    store.start()
                    stores.append(store)
        done = ready
    for store in stores:
        store.wait()


def call(kernel, outs, scratch, args, in_space=pltpu.VMEM, out_space=pltpu.VMEM):
    placed = [pltpu.with_memory_space_constraint(arg, in_space) for arg in args]
    return pl.pallas_call(
        kernel,
        out_shape=[out_space(shape, dtype) for shape, dtype in outs],
        in_specs=[pl.BlockSpec(memory_space=in_space)] * len(args),
        out_specs=[pl.BlockSpec(memory_space=out_space)] * len(outs),
        scratch_shapes=scratch,
        compiler_params=pltpu.CompilerParams(vmem_limit_bytes=GRANT),
    )(*placed)


def by_faces(density, vel_x, vel_y, vel_z, z_modes, z_stiffness):
    bx, by, nz = vel_x.shape
    gx, gy = lax.axis_size("gx"), lax.axis_size("gy")
    peers = gx * gy
    each = nz // peers
    lanes = 2 * (bx + by)
    total_x, total_y = gx * bx, gy * by

    pack = Pack(np.float32)
    pack.add("eig_x", np.broadcast_to(wall_eigen(bx)[:, None], (bx, nz)))
    pack.add("eig_y", np.broadcast_to(wall_eigen(by)[:, None], (by, nz)))
    for name, table in zip(FACTORS, local_tables(bx, by)):
        pack.add(name, table)

    near_x, cos_x, sin_x = phase_tables(gy, by)
    near_y, cos_y, sin_y = phase_tables(gx, bx)
    row_x, row_y = np.arange(peers) // gy, np.arange(peers) % gy
    pack.add("far_xc", cos_x[row_y])
    pack.add("far_xs", sin_x[row_y])
    pack.add("far_yc", cos_y[row_x])
    pack.add("far_ys", sin_y[row_x])
    pack.add("line_x", np.broadcast_to(eigen(total_x), (16, total_x)))
    pack.add("line_y", np.broadcast_to(eigen(total_y), (16, total_y)))
    ahead_x, behind_x = edge_rows(gx, bx)
    ahead_y, behind_y = edge_rows(gy, by)
    ux = np.concatenate([ahead_x[row_x], behind_x[row_x]], 0)
    uy = np.concatenate([ahead_y[row_y], behind_y[row_y]], 0)
    for name, table in (("near_x", near_x), ("near_y", near_y), ("ux", ux), ("uy", uy)):
        pack.add(name, table)

    args = [
        density, vel_x, vel_y, vel_z, pack.array(), z_stiffness.reshape(1, nz), z_modes,
    ]
    parts = LOADS
    cells = ((bx, by, nz), F32)
    traces = ((peers, each, lanes), F32)
    tables = [
        ((2, GROUP * by, GROUP * by), BF16), ((2, GROUP * bx, GROUP * bx), BF16),
        ((2, by // GROUP, GROUP * bx, lanes), BF16),
    ]
    later = [
        ((2, by, 2 * total_y), BF16), ((2, 4 * total_y, lanes), BF16), ((2 * total_x, 128), BF16),
        ((2, bx, 2 * total_x), BF16), ((2, 2 * peers, total_y), BF16),
        ((2, 2 * peers, total_x), BF16), ((total_x, 4 * peers), BF16),
        ((2, total_y, 2 * nz), BF16), ((total_x, total_y), F32), ((2, total_x, nz), F32),
    ]
    hat, sent, scale, own, along_y, along_x, back, *kept = call(
        functools.partial(first_kernel, gx, gy, pack, parts, len(args)),
        [cells, traces, cells, ((each, total_y), F32), *tables, *later] + [(arg.shape, arg.dtype) for arg in args],
        [
            pltpu.VMEM((bx, by, nz), F32),
            pltpu.VMEM((bx + by, nz), F32),
            pltpu.VMEM((2, by // GROUP, lanes, GROUP * bx), BF16),
            pltpu.SemaphoreType.DMA((parts, 4)),
            pltpu.SemaphoreType.DMA((len(args) - 4,)),
        ],
        args,
        in_space=pltpu.HBM,
    )
    got = lax.all_to_all(sent, ("gx", "gy"), 0, 0, tiled=True)
    later, kept = kept[: len(later)], kept[len(later) :]
    rho, vx, vy, vz, own_tables, _, zm = kept
    (solved,) = call(
        functools.partial(middle_kernel, gx, gy, bx, by, pack),
        [traces],
        [],
        (got, own, own_tables, *later),
    )
    flux = lax.all_to_all(solved, ("gx", "gy"), 0, 0, tiled=True)
    block = pltpu.VMEM((bx, by, nz), F32)
    return call(
        functools.partial(last_kernel, gx, gy),
        [cells] * 3,
        [block] * 4 + [pltpu.SemaphoreType.DMA((bx // GROUP, 3))],
        (flux, hat, scale, rho, vx, vy, vz, zm, along_y, along_x, back),
        out_space=pltpu.HBM,
    )


def from_behind(block, axis, distance):
    devices = range(lax.axis_size(axis))
    route = [(i - distance, i) for i in devices if i - distance in devices]
    return lax.ppermute(block, axis, route)


def cosine_table(length):
    rows = lax.broadcasted_iota(jnp.int32, (length, length), 0)
    cols = lax.broadcasted_iota(jnp.int32, (length, length), 1)
    phase = rows * (2 * cols + 1) % (4 * length)
    angle = phase.astype(jnp.float32) * (math.pi / (2 * length))
    scales = jnp.where(rows == 0, math.sqrt(1.0 / length), math.sqrt(2.0 / length))
    return scales * jnp.cos(angle)


def upper_step(values):
    padding = [(0, 0)] * (values.ndim - 1) + [(0, 1)]
    return jnp.pad(values[..., 1:], padding) - values


def lower_step(values):
    padding = [(0, 0)] * (values.ndim - 1) + [(1, 0)]
    return values - jnp.pad(values[..., :-1], padding)


def eigenvalues(modes, length):
    return -(2.0 - 2.0 * jnp.cos(jnp.pi * modes / length))


def by_transposes(density, vel_x, vel_y, vel_z, z_modes, z_stiffness):
    cells_x = vel_x.shape[0]
    cells_y = vel_x.shape[1]
    depth = vel_x.shape[2]
    groups_x = lax.axis_size("gx")
    groups_y = lax.axis_size("gy")
    total_x = cells_x * groups_x
    total_y = cells_y * groups_y
    planes_dev = depth // groups_x
    xmodes_dev = total_x // groups_y
    table_x = cosine_table(total_x)
    table_y = cosine_table(total_y)
    heaviness = density.astype(jnp.float32)
    momentum_x = heaviness * vel_x
    momentum_y = heaviness * vel_y
    momentum_z = heaviness * vel_z
    below_x = from_behind(momentum_x[cells_x - 1 :], "gx", 1)
    below_y = from_behind(momentum_y[:, cells_y - 1 :], "gy", 1)
    diff_x = momentum_x - jnp.concatenate([below_x, momentum_x[:-1]], 0)
    diff_y = momentum_y - jnp.concatenate([below_y, momentum_y[:, :-1]], 1)
    source = diff_x + diff_y + lower_step(momentum_z)
    vertical = jnp.dot(source.reshape(cells_x * cells_y, depth), z_modes, precision=HIGHEST)
    vertical = vertical.reshape(cells_x, cells_y, groups_x, planes_dev).transpose(0, 2, 1, 3)
    vertical = vertical.reshape(cells_x, groups_x, cells_y * planes_dev)
    lines_x = lax.all_to_all(vertical, "gx", split_axis=1, concat_axis=0, tiled=True)
    lines_x = lines_x.reshape(total_x, cells_y, planes_dev)
    mixed = jnp.einsum("xyk,ax->yak", lines_x, table_x, precision=HIGHEST)
    mixed = mixed.reshape(cells_y, groups_y, xmodes_dev * planes_dev)
    lines_y = lax.all_to_all(mixed, "gy", split_axis=1, concat_axis=0, tiled=True)
    right_side = lines_y.reshape(total_y, xmodes_dev * planes_dev)
    spectrum = jnp.dot(table_y, right_side, precision=HIGHEST)
    z_first = lax.axis_index("gx") * planes_dev
    stiff_dev = lax.dynamic_slice_in_dim(z_stiffness, z_first, planes_dev)
    x_first = lax.axis_index("gy") * xmodes_dev
    modes_x = (x_first + jnp.arange(xmodes_dev, dtype=jnp.int32)).astype(jnp.float32)
    modes_y = jnp.arange(total_y, dtype=jnp.int32).astype(jnp.float32)
    divisor = (
        eigenvalues(modes_x, total_x)[None, :, None]
        + eigenvalues(modes_y, total_y)[:, None, None]
        - stiff_dev[None, None, :]
    )
    pressure_hat = spectrum / divisor.reshape(total_y, xmodes_dev * planes_dev)
    y_space = jnp.einsum("by,bc->yc", table_y, pressure_hat, precision=HIGHEST)
    modes_split = z_modes.reshape(depth, groups_x, planes_dev)
    sent_y = y_space.reshape(total_y, 1, xmodes_dev * planes_dev)
    lines_back = lax.all_to_all(sent_y, "gy", split_axis=0, concat_axis=1, tiled=True)
    lines_back = lines_back.reshape(cells_y, total_x, planes_dev)
    space_x = jnp.einsum("yak,ax->xyk", lines_back, table_x, precision=HIGHEST)
    sent_x = space_x.reshape(total_x, 1, cells_y * planes_dev)
    blocks = lax.all_to_all(sent_x, "gx", split_axis=0, concat_axis=1, tiled=True)
    blocks = blocks.reshape(cells_x, groups_x, cells_y, planes_dev)
    pressure = jnp.einsum("xhyk,zhk->xyz", blocks, modes_split, precision=HIGHEST)
    rim_x = from_behind(pressure[0:1], "gx", -1)
    grad_x = jnp.concatenate([pressure[1:], rim_x], 0) - pressure
    rim_y = from_behind(pressure[:, 0:1], "gy", -1)
    grad_y = jnp.concatenate([pressure[:, 1:], rim_y], 1) - pressure
    grad_z = upper_step(pressure)
    new_x = vel_x - grad_x / heaviness
    new_y = vel_y - grad_y / heaviness
    new_z = vel_z - grad_z / heaviness
    return (new_x, new_y, new_z)


def solution(mesh):
    sizes = mesh.shape
    peers = sizes["gx"] * sizes["gy"]

    def local(density, vel_x, vel_y, vel_z, z_modes, z_stiffness):
        cells_x, cells_y, depth = vel_x.shape
        total_x, total_y = cells_x * sizes["gx"], cells_y * sizes["gy"]
        fits = depth % peers == 0 and depth % 128 == 0 and 4 * peers % 128 == 0
        fits = fits and cells_x % (2 * GROUP) == 0 and cells_y % (2 * GROUP) == 0
        fits = fits and total_x % 128 == 0 and total_y % 128 == 0 and 3 * cells_x <= 128
        fits = fits and 2 * (cells_x + cells_y) % 128 == 0
        plan = by_faces if fits else by_transposes
        return tuple(plan(density, vel_x, vel_y, vel_z, z_modes, z_stiffness))

    block = P("gx", "gy", None)
    return jax.shard_map(
        local,
        mesh=mesh,
        in_specs=(block, block, block, block, P(), P()),
        out_specs=(block, block, block),
        check_vma=False,
    )
```
